128 devices in a mesh: row: 8 (over x, core), col: 16 (over z, y).
Axes of the slice: x: 4, y: 4, z: 4, core: 2. Of those that a mesh axis runs over, the one named last changes fastest.
Arguments:
- observed: bfloat16 [4096, 8, 128, 128], P(('row', 'col')), may hold values from -6 to 6
- sku_ids: int32 [4096], P(('row', 'col')), may hold values from 0 to 15
- store_ids: int32 [4096, 8], P(('row', 'col')), may hold values from 0 to 79
- live_slot_counts: int32 [8, 16, 8], P('row', 'col'), may hold values from 0 to 4, as said below
- sku_factors: float32 [262144, 256], P(('row', 'col')), may hold values from -1.5 to 1.5
- store_factors: float32 [81920, 256], P(('row', 'col')), may hold values from -1.5 to 1.5
Outputs:
- new_sku_factors: float32 [262144, 256], P(('row', 'col'))
- new_store_factors: float32 [81920, 256], P(('row', 'col'))
The draws below stay inside these ranges and needn't reach their ends.
Inputs may be any that keep to these rules, and one draw needn't show every extreme that they name: `live_slot_counts`: in every column index some owner row's slots are full from every device of that column.
All inputs are finite; a program needn't handle non-finite values.
Results may differ from the reference program's by a relative error of at most 0.023.
Values may be sent and summed in bfloat16 or wider, within the bound.
A program may use at most 192 MiB of HBM per device.

```python
import jax
import jax.numpy as jnp
from jax import lax

R = 256
BS = 128
K = 8
SLOT_CAPACITY = 4
UB_DEV = 16
VB_DEV = 5
SLOT_ROWS = 4096
VG = 80
NSKU = 262144
NSTORE = 81920
N_ROW = 8
N_COL = 16


def draw_live_slot_counts(key, part):
    first_key = jax.random.fold_in(key, 11)
    second_key = jax.random.fold_in(key, 12)
    busy_key = jax.random.fold_in(key, 13)
    full_key = jax.random.fold_in(key, 14)
    first = jax.random.randint(first_key, (N_ROW, N_COL, N_ROW), 0, SLOT_CAPACITY + 1)
    second = jax.random.randint(second_key, (N_ROW, N_COL, N_ROW), 0, SLOT_CAPACITY + 1)
    busy = jax.random.randint(busy_key, (1, N_COL, N_ROW), 0, 2)
    counts = jnp.where(busy == 1, jnp.maximum(first, second), jnp.minimum(first, second))
    full_owner = jax.random.randint(full_key, (1, N_COL, 1), 0, N_ROW)
    owner_index = lax.broadcasted_iota(jnp.int32, (N_ROW, N_COL, N_ROW), 2)
    return jnp.where(owner_index == full_owner, SLOT_CAPACITY, counts).astype(jnp.int32)


def set_ends(result, key, low, top_value):
    spot = [jax.random.randint(jax.random.fold_in(key, axis), (), 0, length) for axis, length in enumerate(result.shape)]
    main_axis = result.shape.index(max(result.shape))
    neighbour = spot[:main_axis] + [(spot[main_axis] + 1) % result.shape[main_axis]] + spot[main_axis + 1:]
    return result.at[tuple(spot)].set(low).at[tuple(neighbour)].set(top_value)


def shard_levels(key, shape, shards, low, high):
    level = 1.0
    for dim, parts in shards:
        steps = jax.random.uniform(jax.random.fold_in(jax.random.fold_in(key, 6), dim), (parts,), jnp.float32, low / len(shards), high / len(shards))
        level = level * jnp.repeat(jnp.exp(steps), shape[dim] // parts).reshape((-1,) + (1,) * (len(shape) - 1 - dim))
    return level


def noise(key, dims, width, limit, cuts=(), kind=jnp.bfloat16):
    array = width * jax.random.normal(key, dims, jnp.float32)
    if cuts:
        array = array * shard_levels(key, dims, cuts, -0.22, 0.18)
    return jnp.clip(array, -limit, limit).astype(kind)


def setup_inputs(seed: int = 0) -> dict:
    seeds = jax.random.split(jax.random.key(seed), 7)
    observed = noise(seeds[0], (SLOT_ROWS, K, BS, BS), 1.0, 6.0, ((0, 128),))
    sku_ids = set_ends(jax.random.randint(seeds[1], (SLOT_ROWS,), 0, UB_DEV), jax.random.fold_in(seeds[1], 1), 0, UB_DEV - 1).astype(jnp.int32)
    store_ids = set_ends(jax.random.randint(seeds[2], (SLOT_ROWS, K), 0, VG), jax.random.fold_in(seeds[2], 1), 0, VG - 1).astype(jnp.int32)
    live_slot_counts = draw_live_slot_counts(jax.random.fold_in(seeds[6], 71), 0)
    sku_factors = noise(seeds[4], (NSKU, R), 0.25, 1.5, ((0, 128),), jnp.float32)
    store_factors = noise(seeds[5], (NSTORE, R), 0.25, 1.5, ((0, 128),), jnp.float32)
    return {"observed": observed, "sku_ids": sku_ids, "store_ids": store_ids, "live_slot_counts": live_slot_counts, "sku_factors": sku_factors, "store_factors": store_factors}


learn_rate = 0.01
weight_decay = 0.05


def reference(observed, sku_ids, store_ids, live_slot_counts, sku_factors, store_factors):
    total_live_slots = SLOT_CAPACITY * N_ROW
    all_slots = total_live_slots * N_ROW * N_COL
    position = jnp.arange(all_slots, dtype=jnp.int32)
    device = position // total_live_slots
    within_owner = position % total_live_slots
    owner_row = within_owner // SLOT_CAPACITY
    row_of = device // N_COL
    col_of = device % N_COL
    counts_flat = live_slot_counts.reshape(N_ROW * N_COL, N_ROW)
    slot_limits = counts_flat[device, owner_row]
    slot_alive_mask = (within_owner % SLOT_CAPACITY < slot_limits).astype(jnp.float32)
    product_global_index = ((owner_row * N_COL + col_of) * UB_DEV + sku_ids).astype(jnp.int32)
    shop_global_index = (row_of[:, None] * (VB_DEV * N_COL) + store_ids).astype(jnp.int32)
    sku_blocks = sku_factors.reshape(-1, BS, R)
    store_blocks = store_factors.reshape(-1, BS, R)
    sku_low = sku_blocks.astype(jnp.bfloat16)
    store_low = store_blocks.astype(jnp.bfloat16)
    groups = all_slots // 8

    def split_into_groups(array_in):
        return array_in.reshape((groups, 8) + array_in.shape[1:])

    input_arrays = (split_into_groups(product_global_index), split_into_groups(shop_global_index), split_into_groups(observed), split_into_groups(slot_alive_mask))

    def misfit_of(sku_pick, store_pick, measured, store_table):
        selected_rows = sku_low[sku_pick].astype(jnp.float32)
        selected_cols = store_table[store_pick].astype(jnp.float32)
        predicted = jnp.einsum("sar,skbr->skab", selected_rows, selected_cols, precision=lax.Precision.HIGHEST)
        misfit = (predicted - measured.astype(jnp.float32)).astype(jnp.bfloat16)
        misfit = lax.optimization_barrier(misfit).astype(jnp.float32)
        return misfit, selected_rows, selected_cols

    def first_pass(running, inputs_now):
        sku_pick, store_pick, measured, alive = inputs_now
        misfit, selected_rows, selected_cols = misfit_of(sku_pick, store_pick, measured, store_low)
        partial_value = jnp.einsum("skab,sar->skbr", misfit, selected_rows, precision=lax.Precision.HIGHEST)
        partial_value = partial_value * alive[:, None, None, None]
        running = running.at[store_pick.reshape(-1)].add(partial_value.reshape(-1, BS, R))
        return running, None

    store_grad, _ = lax.scan(first_pass, jnp.zeros(store_blocks.shape, jnp.float32), input_arrays)
    new_store = store_blocks - learn_rate * (store_grad + weight_decay * store_blocks)
    new_store_low = new_store.astype(jnp.bfloat16)

    def second_pass(running, inputs_now):
        sku_pick, store_pick, measured, alive = inputs_now
        misfit, selected_rows, selected_cols = misfit_of(sku_pick, store_pick, measured, new_store_low)
        partial_value = jnp.einsum("skab,skbr->sar", misfit, selected_cols, precision=lax.Precision.HIGHEST)
        partial_value = partial_value * alive[:, None, None]
        running = running.at[sku_pick].add(partial_value)
        return running, None

    sku_grad, _ = lax.scan(second_pass, jnp.zeros(sku_blocks.shape, jnp.float32), input_arrays)
    new_sku = sku_blocks - learn_rate * (sku_grad + weight_decay * sku_blocks)
    return new_sku.reshape(sku_factors.shape), new_store.reshape(store_factors.shape)
```

```python
import jax
import jax.numpy as jnp
from jax import lax
from jax.experimental import pallas as pl
from jax.experimental.pallas import tpu as pltpu
from jax.sharding import PartitionSpec as P

learn_rate = 0.01
weight_decay = 0.05
BS = 128
R = 256
K = 8
CAP = 4
N_ROW = 8
SLOTS = 32
UB = 16
VB = 5
VG = 80
DEPTH = 4
VMEM_MOST = 60 * 1024 * 1024

NT = (((1,), (1,)), ((), ()))
f32 = jnp.float32
bf16 = jnp.bfloat16


def live_list(counts, order):
    total = jnp.int32(0)
    for o in range(N_ROW):
        for t in range(CAP):
            order[total] = o * CAP + t
            total = total + (t < counts[o]).astype(jnp.int32)
    return total


def misfit_pair(x, store, first, second, obs, k):
    two = jnp.concatenate([store[first], store[second]], axis=0)
    predicted = lax.dot_general(x, two, NT, preferred_element_type=f32)
    measured = jnp.concatenate([obs[k], obs[k + 1]], axis=1)
    return (predicted - measured.astype(f32)).astype(bf16), two


def first_pass(ids, sku_ids, counts, tables, obs, store, out, acc, order, sku_buf, obs_buf, sem):
    total = live_list(counts, order)

    def copies(i):
        s = order[i]
        at = lax.rem(i, DEPTH)
        return (
            pltpu.make_async_copy(tables.at[s // CAP * UB + sku_ids[s]], sku_buf.at[at], sem.at[0, at]),
            pltpu.make_async_copy(obs.at[s], obs_buf.at[at], sem.at[1, at]),
        )

    for i in range(DEPTH - 1):

        @pl.when(i < total)
        def _():
            for c in copies(i):
                c.start()

    acc[...] = jnp.zeros_like(acc)

    @pl.loop(0, total)
    def _(i):
        @pl.when(i + DEPTH - 1 < total)
        def _():
            for c in copies(i + DEPTH - 1):
                c.start()

        for c in copies(i):
            c.wait()
        s = order[i]
        at = lax.rem(i, DEPTH)
        x = sku_buf[at]
        xt = x.T
        now = obs_buf.at[at]
        for k in range(0, K, 2):
            a, b = ids[s, k], ids[s, k + 1]
            misfit, _ = misfit_pair(x, store, a, b, now, k)
            g = jnp.dot(xt, misfit, preferred_element_type=f32)
            acc[a] += g[:, :BS]
            acc[b] += g[:, BS:]

    out[...] = acc[...].astype(bf16)


def second_pass(ids, sku_ids, counts, tables, obs, store, out, order, sku_buf, obs_buf, sem):
    total = live_list(counts, order)

    def copies(i):
        s = order[i]
        at = lax.rem(i, DEPTH)
        return (
            pltpu.make_async_copy(tables.at[s // CAP * UB + sku_ids[s]], sku_buf.at[at], sem.at[0, at]),
            pltpu.make_async_copy(obs.at[s], obs_buf.at[at], sem.at[1, at]),
        )

    for i in range(DEPTH - 1):

        @pl.when(i < total)
        def _():
            for c in copies(i):
                c.start()

    out[...] = jnp.zeros_like(out)

    @pl.loop(0, total)
    def _(i):
        @pl.when(i + DEPTH - 1 < total)
        def _():
            for c in copies(i + DEPTH - 1):
                c.start()

        for c in copies(i):
            c.wait()
        s = order[i]
        at = lax.rem(i, DEPTH)
        x = sku_buf[at]
        now = obs_buf.at[at]
        g = jnp.zeros((BS, R), f32)
        for k in range(0, K, 2):
            misfit, two = misfit_pair(x, store, ids[s, k], ids[s, k + 1], now, k)
            g = g + jnp.dot(misfit, two, preferred_element_type=f32)
        out[s] = g.astype(bf16)


def last_step(requested, arrived, own, out, acc):
    acc[...] = jnp.zeros_like(acc)

    @pl.loop(0, SLOTS)
    def _(q):
        acc[requested[q]] += arrived[q].astype(f32)

    out[...] = own[...] - learn_rate * (acc[...] + weight_decay * own[...])


SMEM = pl.BlockSpec(memory_space=pltpu.SMEM)
VMEM = pl.BlockSpec(memory_space=pltpu.VMEM)
ANY = pl.BlockSpec(memory_space=pl.ANY)
params = pltpu.CompilerParams(vmem_limit_bytes=VMEM_MOST)


def local(observed, sku_ids, store_ids, live_slot_counts, sku_factors, store_factors):
    counts = live_slot_counts.reshape(N_ROW)
    own_sku = sku_factors.reshape(UB, BS, R)
    own_store = store_factors.reshape(VB, BS, R)
    tables = lax.all_gather(own_sku.astype(bf16), "row", axis=0, tiled=True)
    group_low = lax.all_gather(own_store.astype(bf16), "col", axis=0, tiled=True)
    slot_bufs = [
        pltpu.SMEM((SLOTS + 1,), jnp.int32),
        pltpu.VMEM((DEPTH, BS, R), bf16),
        pltpu.VMEM((DEPTH, K, BS, BS), bf16),
        pltpu.SemaphoreType.DMA((2, DEPTH)),
    ]
    grad = pl.pallas_call(
        first_pass,
        out_shape=jax.ShapeDtypeStruct((VG, R, BS), bf16),
        in_specs=[SMEM, SMEM, SMEM, ANY, ANY, VMEM],
        out_specs=VMEM,
        scratch_shapes=[pltpu.VMEM((VG, R, BS), f32)] + slot_bufs,
        compiler_params=params,
        name="first_pass",
    )(store_ids, sku_ids, counts, tables, observed, group_low)
    own_grad = lax.psum_scatter(grad, "col", scatter_dimension=0, tiled=True).astype(f32)
    own_grad = own_grad.transpose(0, 2, 1)
    new_store = own_store - learn_rate * (own_grad + weight_decay * own_store)
    new_low = lax.all_gather(new_store.astype(bf16), "col", axis=0, tiled=True)
    terms = pl.pallas_call(
        second_pass,
        out_shape=jax.ShapeDtypeStruct((SLOTS, BS, R), bf16),
        in_specs=[SMEM, SMEM, SMEM, ANY, ANY, VMEM],
        out_specs=VMEM,
        scratch_shapes=slot_bufs,
        compiler_params=params,
        name="second_pass",
    )(store_ids, sku_ids, counts, tables, observed, new_low)
    arrived = lax.all_to_all(
        terms.reshape(N_ROW, CAP, BS, R), "row", split_axis=0, concat_axis=0, tiled=True
    )
    requested = lax.all_to_all(
        sku_ids.reshape(N_ROW, CAP), "row", split_axis=0, concat_axis=0, tiled=True
    )
    new_sku = pl.pallas_call(
        last_step,
        out_shape=jax.ShapeDtypeStruct((UB, BS, R), f32),
        in_specs=[SMEM, VMEM, VMEM],
        out_specs=VMEM,
        scratch_shapes=[pltpu.VMEM((UB, BS, R), f32)],
        compiler_params=params,
        name="last_step",
    )(requested.reshape(SLOTS), arrived.reshape(SLOTS, BS, R), own_sku)
    return new_sku.reshape(sku_factors.shape), new_store.reshape(store_factors.shape)


def solution(mesh):
    placed = (
        P(("row", "col"), None, None, None),
        P(("row", "col")),
        P(("row", "col"), None),
        P("row", "col", None),
        P(("row", "col"), None),
        P(("row", "col"), None),
    )
    return jax.shard_map(
        local,
        mesh=mesh,
        in_specs=placed,
        out_specs=(P(("row", "col"), None), P(("row", "col"), None)),
        check_vma=False,
    )
```

```python
import jax
import jax.numpy as jnp
from jax import lax
from jax.experimental import pallas as pl
from jax.experimental.pallas import tpu as pltpu
from jax.sharding import PartitionSpec as P

learn_rate = 0.01
weight_decay = 0.05
BS = 128
R = 256
K = 8
CAP = 4
N_ROW = 8
SLOTS = 32
UB = 16
VB = 5
VG = 80
DEPTH = 4
VMEM_MOST = 60 * 1024 * 1024

RING = 4
MESH = pl.DeviceIdType.MESH
NT = (((1,), (1,)), ((), ()))
f32 = jnp.float32
bf16 = jnp.bfloat16


def live_list(counts, order):
    total = jnp.int32(0)
    for o in range(N_ROW):
        for t in range(CAP):
            order[total] = o * CAP + t
            total = total + (t < counts[o]).astype(jnp.int32)
    return total


def misfit_pair(x, store, first, second, obs, k):
    two = jnp.concatenate([store[first], store[second]], axis=0)
    predicted = lax.dot_general(x, two, NT, preferred_element_type=f32)
    measured = jnp.concatenate([obs[k], obs[k + 1]], axis=1)
    return (predicted - measured.astype(f32)).astype(bf16), two


def first_pass(ids, counts, fetched, obs, store, out, acc, order, sku_buf, obs_buf, sem):
    total = live_list(counts, order)

    def copies(i):
        s = order[i]
        at = lax.rem(i, DEPTH)
        return (
            pltpu.make_async_copy(fetched.at[lax.div(s, CAP), lax.rem(s, CAP)], sku_buf.at[at], sem.at[0, at]),
            pltpu.make_async_copy(obs.at[s], obs_buf.at[at], sem.at[1, at]),
        )

    for i in range(DEPTH - 1):

        @pl.when(i < total)
        def _():
            for c in copies(i):
                c.start()

    acc[...] = jnp.zeros_like(acc)

    @pl.loop(0, total)
    def _(i):
        @pl.when(i + DEPTH - 1 < total)
        def _():
            for c in copies(i + DEPTH - 1):
                c.start()

        for c in copies(i):
            c.wait()
        s = order[i]
        at = lax.rem(i, DEPTH)
        x = sku_buf[at]
        xt = x.T
        now = obs_buf.at[at]
        for k in range(0, K, 2):
            a, b = ids[s, k], ids[s, k + 1]
            misfit, _ = misfit_pair(x, store, a, b, now, k)
            g = jnp.dot(xt, misfit, preferred_element_type=f32)
            acc[a] += g[:, :BS]
            acc[b] += g[:, BS:]

    out[...] = acc[...].astype(bf16)


class Place:
    def __init__(self):
        self.row, self.col = lax.axis_index("row"), lax.axis_index("col")
        self.x, self.core = lax.div(self.row, 2), lax.rem(self.row, 2)
        self.z, self.y = lax.div(self.col, RING), lax.rem(self.col, RING)

    def row_of(self, dx, dc):
        return lax.rem(self.x + dx + RING, RING) * 2 + (1 - self.core if dc else self.core)

    def col_of(self, dy, dz):
        return lax.rem(self.z + dz + RING, RING) * RING + lax.rem(self.y + dy + RING, RING)

    def along_row(self, dx, dc):
        return (self.row_of(dx, dc), self.col)

    def along_col(self, dy, dz):
        return (self.row, self.col_of(dy, dz))


class Wire:
    def __init__(self, send_sem, recv_sem):
        self.send_sem, self.recv_sem, self.made = send_sem, recv_sem, []

    def copy(self, src, dst, to):
        n = len(self.made)
        c = pltpu.make_async_remote_copy(
            src, dst, self.send_sem.at[n], self.recv_sem.at[n], device_id=to, device_id_type=MESH
        )
        c.start()
        self.made.append(c)
        return c

    def finish(self):
        for c in self.made:
            c.wait_send()


def meet(peers):
    barrier = pltpu.get_barrier_semaphore()
    for p in peers:
        pl.semaphore_signal(barrier, inc=1, device_id=p, device_id_type=MESH)
    pl.semaphore_wait(barrier, len(peers))


def col_peers(me):
    return [me.along_col(d, 0) for d in (1, -1)] + [me.along_col(0, d) for d in (1, -1)]


PLACES = [(2, 0), (2, 1), (1, 0), (-1, 0), (1, 1), (-1, 1), (0, 1), (0, 0)]
QUARTER = BS // 4


class Gather:
    def __init__(self, me, wire, own, table):
        self.me, self.wire, self.table = me, wire, table
        self.first, self.second = {}, {}
        for d in (1, -1):
            for h in (0, 1):
                self.first[h, d] = self.send(own, (0, 0), h, 0, 2, self.step(h, 0, d))
        for d in (1, -1):
            for h in (0, 1):
                self.second[h, d, 0, 0] = self.send(own, (0, 0), h, 0, 2, self.step(h, 1, d))

    def step(self, h, phase, d):
        return (d, 0) if h == phase else (0, d)

    def at(self, ref, whole, offset, h, q, n):
        rows = pl.ds((2 * h + q) * QUARTER, n * QUARTER)
        if not whole:
            return ref.at[:, rows, :]
        return ref.at[pl.ds(self.me.col_of(*offset) * VB, VB), rows, :]

    def send(self, own, offset, h, q, n, to):
        src = self.at(own, False, offset, h, q, n) if own is not None else self.at(self.table, True, offset, h, q, n)
        return self.wire.copy(src, self.at(self.table, True, offset, h, q, n), self.me.along_col(*to))

    def middle(self):
        opposite = {}
        for d in (1, -1):
            for h in (0, 1):
                self.first[h, d].wait_recv()
                offset = self.step(h, 0, -d)
                q = 0 if d == 1 else 1
                opposite[h, d] = self.send(None, offset, h, q, 1, self.step(h, 0, d))
                for e in (1, -1):
                    self.second[h, e, -d, 0] = self.send(None, offset, h, 0, 2, self.step(h, 1, e))
        for d in (1, -1):
            for h in (0, 1):
                opposite[h, d].wait_recv()
                q = 0 if d == 1 else 1
                for e in (1, -1):
                    self.second[h, e, 2, q] = self.send(
                        None, self.step(h, 0, 2), h, q, 1, self.step(h, 1, e)
                    )

    def end(self):
        last = []
        for f in (0, -1, 1, 2):
            for e in (1, -1):
                for h in (0, 1):
                    if f == 2:
                        self.second[h, e, 2, 0].wait_recv()
                        self.second[h, e, 2, 1].wait_recv()
                    else:
                        self.second[h, e, f, 0].wait_recv()
                    a, b = self.step(h, 0, f), self.step(h, 1, -e)
                    q = 0 if e == 1 else 1
                    last.append(self.send(None, (a[0] + b[0], a[1] + b[1]), h, q, 1, self.step(h, 1, e)))
        for c in last:
            c.wait_recv()


class Exchange:
    def __init__(self, me, wire, send, recv, relay):
        self.me, self.wire, self.send, self.recv, self.relay = me, wire, send, recv, relay
        self.legs, self.got = {}, []

    def start(self, j):
        dx, dc = PLACES[j]
        me = self.me
        if dx == 2:
            for way, d in ((0, 1), (1, -1)):
                self.legs[way, dc] = self.wire.copy(
                    self.send.at[j, pl.ds(2 * way, 2)], self.relay.at[way, dc], me.along_row(d, 0)
                )
        elif (dx, dc) != (0, 0):
            self.got.append(
                self.wire.copy(self.send.at[j], self.recv.at[me.row], me.along_row(dx, dc))
            )

    def forward(self):
        me = self.me
        for dc in (0, 1):
            for way, d in ((0, 1), (1, -1)):
                self.legs[way, dc].wait_recv()
                self.got.append(
                    self.wire.copy(
                        self.relay.at[way, dc],
                        self.recv.at[me.row_of(-d, 0), pl.ds(2 * way, 2)],
                        me.along_row(d, dc),
                    )
                )

    def end(self):
        for c in self.got:
            c.wait_recv()


GATHER_COPIES = 44
EXCHANGE_COPIES = 13


def gather_kernel(
    ids, own_sku, own_store, group, fetched, requests,
    sku_v, store_v, low, send, relay, heard, heard_s, sems, send_sem, recv_sem,
):
    me = Place()
    load_store = pltpu.make_async_copy(own_store, store_v, sems.at[0])
    load_sku = pltpu.make_async_copy(own_sku, sku_v, sems.at[1])
    load_store.start()
    load_sku.start()
    peers = [me.along_row(*p) for p in PLACES[:-1]]
    meet(col_peers(me) + peers)
    wire = Wire(send_sem, recv_sem)
    asked = [
        wire.copy(ids.at[me.row_of(*p)], heard.at[me.row], me.along_row(*p)) for p in PLACES[:-1]
    ]
    own_ids = pltpu.make_async_copy(ids.at[me.row], heard.at[me.row], sems.at[2])
    own_ids.start()
    load_store.wait()
    low[...] = store_v[...].astype(bf16)
    gather = Gather(me, wire, low, group)
    keep_low = pltpu.make_async_copy(low, group.at[pl.ds(me.col * VB, VB)], sems.at[3])
    keep_low.start()
    for c in asked:
        c.wait_recv()
    own_ids.wait()
    to_scalars = pltpu.make_async_copy(heard, heard_s, sems.at[4])
    to_scalars.start()
    to_result = pltpu.make_async_copy(heard, requests, sems.at[5])
    to_result.start()
    load_sku.wait()
    to_scalars.wait()
    exchange = Exchange(me, wire, send, fetched, relay)
    for j, p in enumerate(PLACES):
        for t in range(CAP):
            send[j, t] = sku_v[heard_s[me.row_of(*p), 0, t]].astype(bf16)
        exchange.start(j)
    keep_sku = pltpu.make_async_copy(send.at[len(PLACES) - 1], fetched.at[me.row], sems.at[6])
    keep_sku.start()
    gather.middle()
    exchange.forward()
    gather.end()
    exchange.end()
    keep_low.wait()
    keep_sku.wait()
    to_result.wait()
    wire.finish()


def quarter(q):
    return pl.ds(q * (R // 4), R // 4)


class Sum:
    def __init__(self, me, wire, part, own_sum, far, near, far2, near2):
        self.me, self.wire, self.part, self.own_sum = me, wire, part, own_sum
        self.far, self.near, self.far2, self.near2 = far, near, far2, near2

    def axis(self, h, phase, d):
        return (d, 0) if h == phase else (0, d)

    def piece(self, h, f, s):
        a, b = self.axis(h, 0, f), self.axis(h, 1, s)
        return pl.ds(self.me.col_of(a[0] + b[0], a[1] + b[1]) * VB, VB)

    def start(self, source):
        me, wire = self.me, self.wire
        self.f_far, self.f_near = {}, {}
        for n, s in enumerate((2, 1, -1, 0)):
            for h in (0, 1):
                for w, d in ((0, 1), (1, -1)):
                    q = quarter(2 * h + w)
                    self.f_far[h, w, n] = wire.copy(
                        source.at[self.piece(h, 2, s), q, :], self.far.at[h, w, n], me.along_col(*self.axis(h, 0, d))
                    )
        for n, s in enumerate((2, 1, -1, 0)):
            for h in (0, 1):
                for w, d in ((0, 1), (1, -1)):
                    other = 1 - w
                    self.f_near[h, w, n, other] = wire.copy(
                        source.at[self.piece(h, d, s), quarter(2 * h + other), :],
                        self.near.at[h, w, n, other],
                        me.along_col(*self.axis(h, 0, d)),
                    )

    def rest(self):
        me, wire, part = self.me, self.wire, self.part
        for n, s in enumerate((2, 1, -1, 0)):
            for h in (0, 1):
                for w, d in ((0, 1), (1, -1)):
                    self.f_far[h, w, n].wait_recv()
                    at, q = self.piece(h, d, s), quarter(2 * h + w)
                    part[at, q, :] = (part[at, q, :].astype(f32) + self.far[h, w, n].astype(f32)).astype(bf16)
                    self.f_near[h, w, n, w] = wire.copy(
                        part.at[at, q, :], self.near.at[h, w, n, w], me.along_col(*self.axis(h, 0, d))
                    )
        s_far, s_near = {}, {}
        for n, s in enumerate((2, 1, -1, 0)):
            for h in (0, 1):
                at = self.piece(h, 0, s)
                for e in (0, 1):
                    for w in (0, 1):
                        self.f_near[h, w, n, e].wait_recv()
                    q = quarter(2 * h + e)
                    total = (
                        part[at, q, :].astype(f32)
                        + self.near[h, 0, n, e].astype(f32)
                        + self.near[h, 1, n, e].astype(f32)
                    )
                    d = 1 if e == 0 else -1
                    to = {1: me.along_col(*self.axis(h, 1, 1)), -1: me.along_col(*self.axis(h, 1, -1))}
                    if s == 2:
                        part[at, q, :] = total.astype(bf16)
                        s_far[h, e] = wire.copy(part.at[at, q, :], self.far2.at[h, e], to[d])
                    elif s == 0:
                        self.own_sum[:, q, :] = total
                    elif s == d:
                        s_far[h, e].wait_recv()
                        part[at, q, :] = (total + self.far2[h, e].astype(f32)).astype(bf16)
                        s_near[h, s, e] = wire.copy(part.at[at, q, :], self.near2.at[h, 0 if s == 1 else 1, e], to[s])
                    else:
                        part[at, q, :] = total.astype(bf16)
                        s_near[h, s, e] = wire.copy(part.at[at, q, :], self.near2.at[h, 0 if s == 1 else 1, e], to[s])
        for h in (0, 1):
            for e in (0, 1):
                s_near[h, 1, e].wait_recv()
                s_near[h, -1, e].wait_recv()
                self.own_sum[:, quarter(2 * h + e), :] += self.near2[h, 0, e].astype(f32) + self.near2[h, 1, e].astype(f32)


SUM_COPIES = 60


def step_kernel(
    ids, counts, grad, fetched, obs, own_store, new_store, arrived,
    part, own_sum, far, near, far2, near2, store_v, table, fetched_v, obs_v, terms, relay,
    sems, send_sem, recv_sem,
):
    me = Place()
    load_store = pltpu.make_async_copy(own_store, store_v, sems.at[0])
    load_part = pltpu.make_async_copy(grad, part, sems.at[1])
    load_store.start()
    load_part.start()
    peers = [me.along_row(*p) for p in PLACES[2:-1]]
    meet(col_peers(me) + peers)
    wire = Wire(send_sem, recv_sem)
    total = Sum(me, wire, part, own_sum, far, near, far2, near2)
    total.start(grad)
    load_part.wait()
    load_fetched = pltpu.make_async_copy(fetched, fetched_v, sems.at[2])
    load_fetched.start()
    load_obs = pltpu.make_async_copy(obs, obs_v, sems.at[3])
    load_obs.start()
    total.rest()
    load_store.wait()
    for v in range(VB):
        was = store_v[v]
        now = was - learn_rate * (own_sum[v].T + weight_decay * was)
        store_v[v] = now
        table[me.col * VB + v] = now.astype(bf16)
    gather = Gather(me, wire, None, table)
    keep_store = pltpu.make_async_copy(store_v, new_store, sems.at[4])
    keep_store.start()
    gather.middle()
    gather.end()
    load_fetched.wait()
    load_obs.wait()
    exchange = Exchange(me, wire, terms, arrived, relay)
    for j, p in enumerate(PLACES):
        o = me.row_of(*p)

        @pl.loop(0, CAP)
        def _(t):
            s = o * CAP + t
            x = fetched_v[o, t]
            now = obs_v.at[s]
            g = jnp.zeros((BS, R), f32)
            for k in range(0, K, 2):
                misfit, two = misfit_pair(x, table, ids[s, k], ids[s, k + 1], now, k)
                g = g + jnp.dot(misfit, two, preferred_element_type=f32)
            terms[j, t] = (g * (t < counts[o]).astype(f32)).astype(bf16)

        exchange.start(j)
        if j == 5:
            exchange.forward()
    keep_sku = pltpu.make_async_copy(terms.at[len(PLACES) - 1], arrived.at[me.row], sems.at[5])
    keep_sku.start()
    exchange.end()
    keep_sku.wait()
    keep_store.wait()
    wire.finish()


def last_step(requested, arrived, own, out, acc):
    acc[...] = jnp.zeros_like(acc)

    @pl.loop(0, SLOTS)
    def _(q):
        acc[requested[lax.div(q, CAP), 0, lax.rem(q, CAP)]] += arrived[q].astype(f32)

    out[...] = own[...] - learn_rate * (acc[...] + weight_decay * own[...])


SMEM = pl.BlockSpec(memory_space=pltpu.SMEM)
VMEM = pl.BlockSpec(memory_space=pltpu.VMEM)
ANY = pl.BlockSpec(memory_space=pl.ANY)
params = pltpu.CompilerParams(vmem_limit_bytes=VMEM_MOST)


def remote_params(n):
    return pltpu.CompilerParams(vmem_limit_bytes=VMEM_MOST, collective_id=n, has_side_effects=True)


def local(observed, sku_ids, store_ids, live_slot_counts, sku_factors, store_factors):
    counts = live_slot_counts.reshape(N_ROW)
    own_sku = sku_factors.reshape(UB, BS, R)
    own_store = store_factors.reshape(VB, BS, R)
    ids = jnp.pad(sku_ids.reshape(N_ROW, 1, CAP), ((0, 0), (0, 7), (0, 124)))
    group_low, fetched, requested = pl.pallas_call(
        gather_kernel,
        out_shape=(
            jax.ShapeDtypeStruct((VG, BS, R), bf16),
            jax.ShapeDtypeStruct((N_ROW, CAP, BS, R), bf16),
            jax.ShapeDtypeStruct((N_ROW, 8, 128), jnp.int32),
        ),
        in_specs=[VMEM, ANY, ANY],
        out_specs=(ANY, ANY, ANY),
        scratch_shapes=[
            pltpu.VMEM((UB, BS, R), f32),
            pltpu.VMEM((VB, BS, R), f32),
            pltpu.VMEM((VB, BS, R), bf16),
            pltpu.VMEM((N_ROW, CAP, BS, R), bf16),
            pltpu.VMEM((2, 2, 2, BS, R), bf16),
            pltpu.VMEM((N_ROW, 8, 128), jnp.int32),
            pltpu.SMEM((N_ROW, 8, 128), jnp.int32),
            pltpu.SemaphoreType.DMA((7,)),
            pltpu.SemaphoreType.DMA((7 + GATHER_COPIES + EXCHANGE_COPIES,)),
            pltpu.SemaphoreType.DMA((7 + GATHER_COPIES + EXCHANGE_COPIES,)),
        ],
        compiler_params=remote_params(0),
        name="gather_kernel",
    )(ids, own_sku, own_store)
    grad = pl.pallas_call(
        first_pass,
        out_shape=jax.ShapeDtypeStruct((VG, R, BS), bf16),
        in_specs=[SMEM, SMEM, ANY, ANY, VMEM],
        out_specs=VMEM,
        scratch_shapes=[
            pltpu.VMEM((VG, R, BS), f32),
            pltpu.SMEM((SLOTS + 1,), jnp.int32),
            pltpu.VMEM((DEPTH, BS, R), bf16),
            pltpu.VMEM((DEPTH, K, BS, BS), bf16),
            pltpu.SemaphoreType.DMA((2, DEPTH)),
        ],
        compiler_params=params,
        name="first_pass",
    )(store_ids, counts, fetched, observed, group_low)
    new_store, arrived = pl.pallas_call(
        step_kernel,
        out_shape=(
            jax.ShapeDtypeStruct((VB, BS, R), f32),
            jax.ShapeDtypeStruct((N_ROW, CAP, BS, R), bf16),
        ),
        in_specs=[SMEM, SMEM, ANY, ANY, ANY, ANY],
        out_specs=(ANY, ANY),
        scratch_shapes=[
            pltpu.VMEM((VG, R, BS), bf16),
            pltpu.VMEM((VB, R, BS), f32),
            pltpu.VMEM((2, 2, RING, VB, R // 4, BS), bf16),
            pltpu.VMEM((2, 2, RING, 2, VB, R // 4, BS), bf16),
            pltpu.VMEM((2, 2, VB, R // 4, BS), bf16),
            pltpu.VMEM((2, 2, 2, VB, R // 4, BS), bf16),
            pltpu.VMEM((VB, BS, R), f32),
            pltpu.VMEM((VG, BS, R), bf16),
            pltpu.VMEM((N_ROW, CAP, BS, R), bf16),
            pltpu.VMEM((SLOTS, K, BS, BS), bf16),
            pltpu.VMEM((N_ROW, CAP, BS, R), bf16),
            pltpu.VMEM((2, 2, 2, BS, R), bf16),
            pltpu.SemaphoreType.DMA((6,)),
            pltpu.SemaphoreType.DMA((SUM_COPIES + GATHER_COPIES + EXCHANGE_COPIES,)),
            pltpu.SemaphoreType.DMA((SUM_COPIES + GATHER_COPIES + EXCHANGE_COPIES,)),
        ],
        compiler_params=remote_params(1),
        name="step_kernel",
    )(store_ids, counts, grad, fetched, observed, own_store)
    new_sku = pl.pallas_call(
        last_step,
        out_shape=jax.ShapeDtypeStruct((UB, BS, R), f32),
        in_specs=[SMEM, VMEM, VMEM],
        out_specs=VMEM,
        scratch_shapes=[pltpu.VMEM((UB, BS, R), f32)],
        compiler_params=params,
        name="last_step",
    )(requested, arrived.reshape(SLOTS, BS, R), own_sku)
    return new_sku.reshape(sku_factors.shape), new_store.reshape(store_factors.shape)


def solution(mesh):
    placed = (
        P(("row", "col"), None, None, None),
        P(("row", "col")),
        P(("row", "col"), None),
        P("row", "col", None),
        P(("row", "col"), None),
        P(("row", "col"), None),
    )
    return jax.shard_map(
        local,
        mesh=mesh,
        in_specs=placed,
        out_specs=(P(("row", "col"), None), P(("row", "col"), None)),
        check_vma=False,
    )
```

```python
import jax
import jax.numpy as jnp
from jax import lax
from jax.experimental import pallas as pl
from jax.experimental.pallas import tpu as pltpu
from jax.sharding import PartitionSpec as P

learn_rate = 0.01
weight_decay = 0.05
BS = 128
R = 256
K = 8
CAP = 4
N_ROW = 8
SLOTS = 32
UB = 16
VB = 5
VG = 80
DEPTH = 4
CHUNKS = 8
VMEM_MOST = 60 * 1024 * 1024

RING = 4
MESH = pl.DeviceIdType.MESH
NT = (((1,), (1,)), ((), ()))
f32 = jnp.float32
bf16 = jnp.bfloat16


def live_list(counts, order):
    total = jnp.int32(0)
    for o in range(N_ROW):
        for t in range(CAP):
            order[total] = o * CAP + t
            total = total + (t < counts[o]).astype(jnp.int32)
    return total


def misfit_pair(x, store, first, second, obs, k):
    two = jnp.concatenate([store[first], store[second]], axis=0)
    predicted = lax.dot_general(x, two, NT, preferred_element_type=f32)
    measured = jnp.concatenate([obs[k], obs[k + 1]], axis=1)
    return (predicted - measured.astype(f32)).astype(bf16), two


def first_pass(
    ids, counts, fetched, obs, group, out,
    store, acc, order, sku_buf, obs_buf, misfits, staged, sem, end_sem,
):
    load_store = pltpu.make_async_copy(group, store, end_sem.at[CHUNKS])
    load_store.start()
    total = live_list(counts, order)

    def copies(i):
        s = order[i]
        at = lax.rem(i, DEPTH)
        return (
            pltpu.make_async_copy(fetched.at[lax.div(s, CAP), lax.rem(s, CAP)], sku_buf.at[at], sem.at[0, at]),
            pltpu.make_async_copy(obs.at[s], obs_buf.at[at], sem.at[1, at]),
        )

    def misfit(i, k):
        s = order[i]
        at = lax.rem(i, DEPTH)
        return misfit_pair(sku_buf[at], store, ids[k, s], ids[k + 1, s], obs_buf.at[at], k)[0]

    for i in range(DEPTH - 1):

        @pl.when(i < total)
        def _():
            for c in copies(i):
                c.start()

    acc[...] = jnp.zeros_like(acc)
    load_store.wait()

    @pl.when(total > 0)
    def _():
        for c in copies(0):
            c.wait()
        for k in range(0, K, 2):
            misfits[k // 2] = misfit(0, k)

    @pl.loop(0, total)
    def _(i):
        @pl.when(i + DEPTH - 1 < total)
        def _():
            for c in copies(i + DEPTH - 1):
                c.start()

        @pl.when(i + 1 < total)
        def _():
            for c in copies(i + 1):
                c.wait()

        s = order[i]
        later = jnp.minimum(i + 1, total - 1)
        xt = sku_buf[lax.rem(i, DEPTH)].T
        for k in range(0, K, 2):
            a, b = ids[k, s], ids[k + 1, s]
            g = jnp.dot(xt, misfits[k // 2], preferred_element_type=f32)
            misfits[k // 2] = misfit(later, k)
            acc[a] += g[:, :BS]
            acc[b] += g[:, BS:]

    n = VG // CHUNKS
    stores = []
    for q in range(CHUNKS):
        part = pl.ds(q * n, n)
        staged[part] = acc[part].astype(bf16)
        c = pltpu.make_async_copy(staged.at[part], out.at[part], end_sem.at[q])
        c.start()
        stores.append(c)
    for c in stores:
        c.wait()


class Place:
    def __init__(self):
        self.row, self.col = lax.axis_index("row"), lax.axis_index("col")
        self.x, self.core = lax.div(self.row, 2), lax.rem(self.row, 2)
        self.z, self.y = lax.div(self.col, RING), lax.rem(self.col, RING)

    def row_of(self, dx, dc):
        return lax.rem(self.x + dx + RING, RING) * 2 + (1 - self.core if dc else self.core)

    def col_of(self, dy, dz):
        return lax.rem(self.z + dz + RING, RING) * RING + lax.rem(self.y + dy + RING, RING)

    def along_row(self, dx, dc):
        return (self.row_of(dx, dc), self.col)

    def along_col(self, dy, dz):
        return (self.row, self.col_of(dy, dz))


class Wire:
    def __init__(self, send_sem, recv_sem):
        self.send_sem, self.recv_sem, self.made = send_sem, recv_sem, []

    def copy(self, src, dst, to):
        n = len(self.made)
        c = pltpu.make_async_remote_copy(
            src, dst, self.send_sem.at[n], self.recv_sem.at[n], device_id=to, device_id_type=MESH
        )
        c.start()
        self.made.append(c)
        return c

    def finish(self):
        for c in self.made:
            c.wait_send()


def meet(peers):
    barrier = pltpu.get_barrier_semaphore()
    for p in peers:
        pl.semaphore_signal(barrier, inc=1, device_id=p, device_id_type=MESH)
    pl.semaphore_wait(barrier, len(peers))


def col_peers(me):
    return [me.along_col(d, 0) for d in (1, -1)] + [me.along_col(0, d) for d in (1, -1)]


PLACES = [(2, 0), (2, 1), (1, 0), (-1, 0), (1, 1), (-1, 1), (0, 1), (0, 0)]
QUARTER = BS // 4


class Gather:
    def __init__(self, me, wire, own, table):
        self.me, self.wire, self.table = me, wire, table
        self.first, self.second = {}, {}
        for d in (1, -1):
            for h in (0, 1):
                self.first[h, d] = self.send(own, (0, 0), h, 0, 2, self.step(h, 0, d))
        for d in (1, -1):
            for h in (0, 1):
                self.second[h, d, 0, 0] = self.send(own, (0, 0), h, 0, 2, self.step(h, 1, d))

    def step(self, h, phase, d):
        return (d, 0) if h == phase else (0, d)

    def at(self, ref, whole, offset, h, q, n):
        rows = pl.ds((2 * h + q) * QUARTER, n * QUARTER)
        if not whole:
            return ref.at[:, rows, :]
        return ref.at[pl.ds(self.me.col_of(*offset) * VB, VB), rows, :]

    def send(self, own, offset, h, q, n, to):
        src = self.at(own, False, offset, h, q, n) if own is not None else self.at(self.table, True, offset, h, q, n)
        return self.wire.copy(src, self.at(self.table, True, offset, h, q, n), self.me.along_col(*to))

    def middle(self):
        opposite = {}
        for d in (1, -1):
            for h in (0, 1):
                self.first[h, d].wait_recv()
                offset = self.step(h, 0, -d)
                q = 0 if d == 1 else 1
                opposite[h, d] = self.send(None, offset, h, q, 1, self.step(h, 0, d))
                for e in (1, -1):
                    self.second[h, e, -d, 0] = self.send(None, offset, h, 0, 2, self.step(h, 1, e))
        for d in (1, -1):
            for h in (0, 1):
                opposite[h, d].wait_recv()
                q = 0 if d == 1 else 1
                for e in (1, -1):
                    self.second[h, e, 2, q] = self.send(
                        None, self.step(h, 0, 2), h, q, 1, self.step(h, 1, e)
                    )

    def end(self):
        last = []
        for f in (0, -1, 1, 2):
            for e in (1, -1):
                for h in (0, 1):
                    if f == 2:
                        self.second[h, e, 2, 0].wait_recv()
                        self.second[h, e, 2, 1].wait_recv()
                    else:
                        self.second[h, e, f, 0].wait_recv()
                    a, b = self.step(h, 0, f), self.step(h, 1, -e)
                    q = 0 if e == 1 else 1
                    last.append(self.send(None, (a[0] + b[0], a[1] + b[1]), h, q, 1, self.step(h, 1, e)))
        for c in last:
            c.wait_recv()


class Exchange:
    def __init__(self, me, wire, send, recv, relay):
        self.me, self.wire, self.send, self.recv, self.relay = me, wire, send, recv, relay
        self.legs, self.got = {}, []

    def start(self, j):
        dx, dc = PLACES[j]
        me = self.me
        if dx == 2:
            for way, d in ((0, 1), (1, -1)):
                self.legs[way, dc] = self.wire.copy(
                    self.send.at[j, pl.ds(2 * way, 2)], self.relay.at[way, dc], me.along_row(d, 0)
                )
        elif (dx, dc) != (0, 0):
            self.got.append(
                self.wire.copy(self.send.at[j], self.recv.at[me.row], me.along_row(dx, dc))
            )

    def forward(self):
        me = self.me
        for dc in (0, 1):
            for way, d in ((0, 1), (1, -1)):
                self.legs[way, dc].wait_recv()
                self.got.append(
                    self.wire.copy(
                        self.relay.at[way, dc],
                        self.recv.at[me.row_of(-d, 0), pl.ds(2 * way, 2)],
                        me.along_row(d, dc),
                    )
                )

    def end(self):
        for c in self.got:
            c.wait_recv()


GATHER_COPIES = 44
EXCHANGE_COPIES = 13


def gather_kernel(
    ids, own_sku, own_store, group, fetched, requests,
    ids_v, sku_v, store_v, low, send, relay, heard, heard_s, sems, send_sem, recv_sem,
):
    me = Place()
    load_store = pltpu.make_async_copy(own_store, store_v, sems.at[0])
    load_sku = pltpu.make_async_copy(own_sku, sku_v, sems.at[1])
    load_store.start()
    load_sku.start()
    ids_v[...] = jnp.zeros_like(ids_v)
    ids_v[0:1, 0:SLOTS] = ids[...]
    peers = [me.along_row(*p) for p in PLACES[:-1]]
    meet(col_peers(me) + peers)
    wire = Wire(send_sem, recv_sem)
    asked = [
        wire.copy(ids_v, heard.at[me.row], me.along_row(*p)) for p in PLACES[:-1]
    ]
    own_ids = pltpu.make_async_copy(ids_v, heard.at[me.row], sems.at[2])
    own_ids.start()
    load_store.wait()
    low[...] = store_v[...].astype(bf16)
    gather = Gather(me, wire, low, group)
    keep_low = pltpu.make_async_copy(low, group.at[pl.ds(me.col * VB, VB)], sems.at[3])
    keep_low.start()
    for c in asked:
        c.wait_recv()
    own_ids.wait()
    to_scalars = pltpu.make_async_copy(heard, heard_s, sems.at[4])
    to_scalars.start()
    to_result = pltpu.make_async_copy(heard, requests, sems.at[5])
    to_result.start()
    load_sku.wait()
    to_scalars.wait()
    exchange = Exchange(me, wire, send, fetched, relay)
    for j, p in enumerate(PLACES):
        for t in range(CAP):
            send[j, t] = sku_v[heard_s[me.row_of(*p), 0, me.row * CAP + t]].astype(bf16)
        exchange.start(j)
    keep_sku = pltpu.make_async_copy(send.at[len(PLACES) - 1], fetched.at[me.row], sems.at[6])
    keep_sku.start()
    gather.middle()
    exchange.forward()
    gather.end()
    exchange.end()
    keep_low.wait()
    keep_sku.wait()
    to_result.wait()
    wire.finish()


def quarter(q):
    return pl.ds(q * (R // 4), R // 4)


class Sum:
    def __init__(self, me, wire, part, own_sum, far, near, far2, near2):
        self.me, self.wire, self.part, self.own_sum = me, wire, part, own_sum
        self.far, self.near, self.far2, self.near2 = far, near, far2, near2

    def axis(self, h, phase, d):
        return (d, 0) if h == phase else (0, d)

    def piece(self, h, f, s):
        a, b = self.axis(h, 0, f), self.axis(h, 1, s)
        return pl.ds(self.me.col_of(a[0] + b[0], a[1] + b[1]) * VB, VB)

    def start(self, source):
        me, wire = self.me, self.wire
        self.f_far, self.f_near = {}, {}
        for n, s in enumerate((2, 1, -1, 0)):
            for h in (0, 1):
                for w, d in ((0, 1), (1, -1)):
                    q = quarter(2 * h + w)
                    self.f_far[h, w, n] = wire.copy(
                        source.at[self.piece(h, 2, s), q, :], self.far.at[h, w, n], me.along_col(*self.axis(h, 0, d))
                    )
        for n, s in enumerate((2, 1, -1, 0)):
            for h in (0, 1):
                for w, d in ((0, 1), (1, -1)):
                    other = 1 - w
                    self.f_near[h, w, n, other] = wire.copy(
                        source.at[self.piece(h, d, s), quarter(2 * h + other), :],
                        self.near.at[h, w, n, other],
                        me.along_col(*self.axis(h, 0, d)),
                    )

    def rest(self):
        me, wire, part = self.me, self.wire, self.part
        for n, s in enumerate((2, 1, -1, 0)):
            for h in (0, 1):
                for w, d in ((0, 1), (1, -1)):
                    self.f_far[h, w, n].wait_recv()
                    at, q = self.piece(h, d, s), quarter(2 * h + w)
                    part[at, q, :] = (part[at, q, :].astype(f32) + self.far[h, w, n].astype(f32)).astype(bf16)
                    self.f_near[h, w, n, w] = wire.copy(
                        part.at[at, q, :], self.near.at[h, w, n, w], me.along_col(*self.axis(h, 0, d))
                    )
        s_far, s_near = {}, {}
        for n, s in enumerate((2, 1, -1, 0)):
            for h in (0, 1):
                at = self.piece(h, 0, s)
                for e in (0, 1):
                    for w in (0, 1):
                        self.f_near[h, w, n, e].wait_recv()
                    q = quarter(2 * h + e)
                    total = (
                        part[at, q, :].astype(f32)
                        + self.near[h, 0, n, e].astype(f32)
                        + self.near[h, 1, n, e].astype(f32)
                    )
                    d = 1 if e == 0 else -1
                    to = {1: me.along_col(*self.axis(h, 1, 1)), -1: me.along_col(*self.axis(h, 1, -1))}
                    if s == 2:
                        part[at, q, :] = total.astype(bf16)
                        s_far[h, e] = wire.copy(part.at[at, q, :], self.far2.at[h, e], to[d])
                    elif s == 0:
                        self.own_sum[:, q, :] = total
                    elif s == d:
                        s_far[h, e].wait_recv()
                        part[at, q, :] = (total + self.far2[h, e].astype(f32)).astype(bf16)
                        s_near[h, s, e] = wire.copy(part.at[at, q, :], self.near2.at[h, 0 if s == 1 else 1, e], to[s])
                    else:
                        part[at, q, :] = total.astype(bf16)
                        s_near[h, s, e] = wire.copy(part.at[at, q, :], self.near2.at[h, 0 if s == 1 else 1, e], to[s])
        for h in (0, 1):
            for e in (0, 1):
                s_near[h, 1, e].wait_recv()
                s_near[h, -1, e].wait_recv()
                self.own_sum[:, quarter(2 * h + e), :] += self.near2[h, 0, e].astype(f32) + self.near2[h, 1, e].astype(f32)


SUM_COPIES = 60


def step_kernel(
    ids, counts, grad, fetched, obs, own_store, new_store, arrived,
    part, own_sum, far, near, far2, near2, store_v, table, fetched_v, obs_v, terms, relay,
    sems, send_sem, recv_sem,
):
    me = Place()
    load_store = pltpu.make_async_copy(own_store, store_v, sems.at[0])
    load_part = pltpu.make_async_copy(grad, part, sems.at[1])
    load_store.start()
    load_part.start()
    peers = [me.along_row(*p) for p in PLACES[2:-1]]
    meet(col_peers(me) + peers)
    wire = Wire(send_sem, recv_sem)
    total = Sum(me, wire, part, own_sum, far, near, far2, near2)
    total.start(grad)
    load_part.wait()
    load_fetched = pltpu.make_async_copy(fetched, fetched_v, sems.at[2])
    load_fetched.start()
    load_obs = pltpu.make_async_copy(obs, obs_v, sems.at[3])
    load_obs.start()
    total.rest()
    load_store.wait()
    for v in range(VB):
        was = store_v[v]
        now = was - learn_rate * (own_sum[v].T + weight_decay * was)
        store_v[v] = now
        table[me.col * VB + v] = now.astype(bf16)
    gather = Gather(me, wire, None, table)
    keep_store = pltpu.make_async_copy(store_v, new_store, sems.at[4])
    keep_store.start()
    gather.middle()
    gather.end()
    load_fetched.wait()
    load_obs.wait()
    exchange = Exchange(me, wire, terms, arrived, relay)
    for j, p in enumerate(PLACES):
        o = me.row_of(*p)

        @pl.loop(0, CAP)
        def _(t):
            s = o * CAP + t
            x = fetched_v[o, t]
            now = obs_v.at[s]
            g = jnp.zeros((BS, R), f32)
            for k in range(0, K, 2):
                misfit, two = misfit_pair(x, table, ids[k, s], ids[k + 1, s], now, k)
                g = g + jnp.dot(misfit, two, preferred_element_type=f32)
            terms[j, t] = (g * (t < counts[o]).astype(f32)).astype(bf16)

        exchange.start(j)
        if j == 5:
            exchange.forward()
    keep_sku = pltpu.make_async_copy(terms.at[len(PLACES) - 1], arrived.at[me.row], sems.at[5])
    keep_sku.start()
    exchange.end()
    keep_sku.wait()
    keep_store.wait()
    wire.finish()


def last_step(requested, arrived, own, store, out, new_store):
    new_store[...] = store[...]
    row = lax.axis_index("row")
    out[...] = own[...] * (1 - learn_rate * weight_decay)

    @pl.loop(0, N_ROW)
    def _(o):
        for t in range(CAP):
            out[requested[o, 0, row * CAP + t]] -= learn_rate * arrived[o * CAP + t].astype(f32)


SMEM = pl.BlockSpec(memory_space=pltpu.SMEM)
VMEM = pl.BlockSpec(memory_space=pltpu.VMEM)
ANY = pl.BlockSpec(memory_space=pl.ANY)
params = pltpu.CompilerParams(vmem_limit_bytes=VMEM_MOST)


def remote_params(n):
    return pltpu.CompilerParams(vmem_limit_bytes=VMEM_MOST, collective_id=n, has_side_effects=True)


def local(observed, sku_ids, store_ids, live_slot_counts, sku_factors, store_factors):
    counts = live_slot_counts.reshape(N_ROW)
    own_sku = sku_factors.reshape(UB, BS, R)
    own_store = store_factors.reshape(VB, BS, R)
    store_ids = store_ids.T
    group_low, fetched, requested = pl.pallas_call(
        gather_kernel,
        out_shape=(
            jax.ShapeDtypeStruct((VG, BS, R), bf16),
            jax.ShapeDtypeStruct((N_ROW, CAP, BS, R), bf16),
            jax.ShapeDtypeStruct((N_ROW, 8, 128), jnp.int32),
        ),
        in_specs=[VMEM, ANY, ANY],
        out_specs=(ANY, ANY, ANY),
        scratch_shapes=[
            pltpu.VMEM((8, 128), jnp.int32),
            pltpu.VMEM((UB, BS, R), f32),
            pltpu.VMEM((VB, BS, R), f32),
            pltpu.VMEM((VB, BS, R), bf16),
            pltpu.VMEM((N_ROW, CAP, BS, R), bf16),
            pltpu.VMEM((2, 2, 2, BS, R), bf16),
            pltpu.VMEM((N_ROW, 8, 128), jnp.int32),
            pltpu.SMEM((N_ROW, 8, 128), jnp.int32),
            pltpu.SemaphoreType.DMA((7,)),
            pltpu.SemaphoreType.DMA((7 + GATHER_COPIES + EXCHANGE_COPIES,)),
            pltpu.SemaphoreType.DMA((7 + GATHER_COPIES + EXCHANGE_COPIES,)),
        ],
        compiler_params=remote_params(0),
        name="gather_kernel",
    )(sku_ids.reshape(1, SLOTS), own_sku, own_store)
    grad = pl.pallas_call(
        first_pass,
        out_shape=jax.ShapeDtypeStruct((VG, R, BS), bf16),
        in_specs=[SMEM, SMEM, ANY, ANY, ANY],
        out_specs=ANY,
        scratch_shapes=[
            pltpu.VMEM((VG, BS, R), bf16),
            pltpu.VMEM((VG, R, BS), f32),
            pltpu.SMEM((SLOTS + 1,), jnp.int32),
            pltpu.VMEM((DEPTH, BS, R), bf16),
            pltpu.VMEM((DEPTH, K, BS, BS), bf16),
            pltpu.VMEM((K // 2, BS, 2 * BS), bf16),
            pltpu.VMEM((VG, R, BS), bf16),
            pltpu.SemaphoreType.DMA((2, DEPTH)),
            pltpu.SemaphoreType.DMA((CHUNKS + 1,)),
        ],
        compiler_params=params,
        name="first_pass",
    )(store_ids, counts, fetched, observed, group_low)
    new_store, arrived = pl.pallas_call(
        step_kernel,
        out_shape=(
            jax.ShapeDtypeStruct((VB, BS, R), f32),
            jax.ShapeDtypeStruct((N_ROW, CAP, BS, R), bf16),
        ),
        in_specs=[SMEM, SMEM, ANY, ANY, ANY, ANY],
        out_specs=(ANY, ANY),
        scratch_shapes=[
            pltpu.VMEM((VG, R, BS), bf16),
            pltpu.VMEM((VB, R, BS), f32),
            pltpu.VMEM((2, 2, RING, VB, R // 4, BS), bf16),
            pltpu.VMEM((2, 2, RING, 2, VB, R // 4, BS), bf16),
            pltpu.VMEM((2, 2, VB, R // 4, BS), bf16),
            pltpu.VMEM((2, 2, 2, VB, R // 4, BS), bf16),
            pltpu.VMEM((VB, BS, R), f32),
            pltpu.VMEM((VG, BS, R), bf16),
            pltpu.VMEM((N_ROW, CAP, BS, R), bf16),
            pltpu.VMEM((SLOTS, K, BS, BS), bf16),
            pltpu.VMEM((N_ROW, CAP, BS, R), bf16),
            pltpu.VMEM((2, 2, 2, BS, R), bf16),
            pltpu.SemaphoreType.DMA((6,)),
            pltpu.SemaphoreType.DMA((SUM_COPIES + GATHER_COPIES + EXCHANGE_COPIES,)),
            pltpu.SemaphoreType.DMA((SUM_COPIES + GATHER_COPIES + EXCHANGE_COPIES,)),
        ],
        compiler_params=remote_params(1),
        name="step_kernel",
    )(store_ids, counts, grad, fetched, observed, own_store)
    part = lambda n: pl.BlockSpec((n, BS // 2, R), lambda i: (0, i, 0))
    new_sku, new_store = pl.pallas_call(
        last_step,
        out_shape=(
            jax.ShapeDtypeStruct((UB, BS, R), f32),
            jax.ShapeDtypeStruct((VB, BS, R), f32),
        ),
        grid=(2,),
        in_specs=[SMEM, part(SLOTS), part(UB), part(VB)],
        out_specs=(part(UB), part(VB)),
        compiler_params=params,
        name="last_step",
    )(requested, arrived.reshape(SLOTS, BS, R), own_sku, new_store)
    return new_sku.reshape(sku_factors.shape), new_store.reshape(store_factors.shape)


def solution(mesh):
    placed = (
        P(("row", "col"), None, None, None),
        P(("row", "col")),
        P(("row", "col"), None),
        P("row", "col", None),
        P(("row", "col"), None),
        P(("row", "col"), None),
    )
    return jax.shard_map(
        local,
        mesh=mesh,
        in_specs=placed,
        out_specs=(P(("row", "col"), None), P(("row", "col"), None)),
        check_vma=False,
    )
```

```python
import jax
import jax.numpy as jnp
from jax import lax
from jax.experimental import pallas as pl
from jax.experimental.pallas import tpu as pltpu
from jax.sharding import PartitionSpec as P

learn_rate = 0.01
weight_decay = 0.05
BS = 128
R = 256
K = 8
CAP = 4
N_ROW = 8
SLOTS = 32
UB = 16
VB = 5
VG = 80
DEPTH = 4
CHUNKS = 8
VMEM_MOST = 60 * 1024 * 1024

RING = 4
MESH = pl.DeviceIdType.MESH
NT = (((1,), (1,)), ((), ()))
f32 = jnp.float32
bf16 = jnp.bfloat16


def live_list(counts, order):
    total = jnp.int32(0)
    for o in range(N_ROW):
        for t in range(CAP):
            order[total] = o * CAP + t
            total = total + (t < counts[o]).astype(jnp.int32)
    return total


def misfit_pair(x, two, obs, k):
    predicted = lax.dot_general(x, two, NT, preferred_element_type=f32)
    measured = jnp.concatenate([obs[k], obs[k + 1]], axis=1)
    return (predicted - measured.astype(f32)).astype(bf16)


def first_pass(
    ids, counts, fetched, obs, group, out,
    store, acc, order, sku_buf, obs_buf, misfits, staged, sem, end_sem,
):
    load_store = pltpu.make_async_copy(group, store, end_sem.at[CHUNKS])
    load_store.start()
    total = live_list(counts, order)

    def copies(i):
        s = order[i]
        at = lax.rem(i, DEPTH)
        return (
            pltpu.make_async_copy(fetched.at[lax.div(s, CAP), lax.rem(s, CAP)], sku_buf.at[at], sem.at[0, at]),
            pltpu.make_async_copy(obs.at[s], obs_buf.at[at], sem.at[1, at]),
        )

    def misfit(i, k):
        s = order[i]
        at = lax.rem(i, DEPTH)
        two = jnp.concatenate([store[ids[k, s]], store[ids[k + 1, s]]], axis=0)
        return misfit_pair(sku_buf[at], two, obs_buf.at[at], k)

    for i in range(DEPTH - 1):

        @pl.when(i < total)
        def _():
            for c in copies(i):
                c.start()

    acc[...] = jnp.zeros_like(acc)
    load_store.wait()

    @pl.when(total > 0)
    def _():
        for c in copies(0):
            c.wait()
        for k in range(0, K, 2):
            misfits[k // 2] = misfit(0, k)

    @pl.loop(0, total)
    def _(i):
        @pl.when(i + DEPTH - 1 < total)
        def _():
            for c in copies(i + DEPTH - 1):
                c.start()

        @pl.when(i + 1 < total)
        def _():
            for c in copies(i + 1):
                c.wait()

        s = order[i]
        later = jnp.minimum(i + 1, total - 1)
        xt = sku_buf[lax.rem(i, DEPTH)].T
        for k in range(0, K, 2):
            a, b = ids[k, s], ids[k + 1, s]
            g = jnp.dot(xt, misfits[k // 2], preferred_element_type=f32)
            misfits[k // 2] = misfit(later, k)
            acc[a] += g[:, :BS]
            acc[b] += g[:, BS:]

    n = VG // CHUNKS
    stores = []
    for q in range(CHUNKS):
        part = pl.ds(q * n, n)
        staged[part] = acc[part].astype(bf16)
        c = pltpu.make_async_copy(staged.at[part], out.at[part], end_sem.at[q])
        c.start()
        stores.append(c)
    for c in stores:
        c.wait()


class Place:
    def __init__(self):
        self.row, self.col = lax.axis_index("row"), lax.axis_index("col")
        self.x, self.core = lax.div(self.row, 2), lax.rem(self.row, 2)
        self.z, self.y = lax.div(self.col, RING), lax.rem(self.col, RING)

    def row_of(self, dx, dc):
        return lax.rem(self.x + dx + RING, RING) * 2 + (1 - self.core if dc else self.core)

    def col_of(self, dy, dz):
        return lax.rem(self.z + dz + RING, RING) * RING + lax.rem(self.y + dy + RING, RING)

    def along_row(self, dx, dc):
        return (self.row_of(dx, dc), self.col)

    def along_col(self, dy, dz):
        return (self.row, self.col_of(dy, dz))


class Wire:
    def __init__(self, send_sem, recv_sem):
        self.send_sem, self.recv_sem, self.made = send_sem, recv_sem, []

    def copy(self, src, dst, to):
        n = len(self.made)
        c = pltpu.make_async_remote_copy(
            src, dst, self.send_sem.at[n], self.recv_sem.at[n], device_id=to, device_id_type=MESH
        )
        c.start()
        self.made.append(c)
        return c

    def finish(self):
        for c in self.made:
            c.wait_send()


def meet(peers):
    barrier = pltpu.get_barrier_semaphore()
    for p in peers:
        pl.semaphore_signal(barrier, inc=1, device_id=p, device_id_type=MESH)
    pl.semaphore_wait(barrier, len(peers))


def col_peers(me):
    return [me.along_col(d, 0) for d in (1, -1)] + [me.along_col(0, d) for d in (1, -1)]


PLACES = [(2, 0), (2, 1), (1, 0), (-1, 0), (1, 1), (-1, 1), (0, 1), (0, 0)]
QUARTER = BS // 4


class Gather:
    def __init__(self, me, wire, own, table):
        self.me, self.wire, self.table = me, wire, table
        self.first, self.second = {}, {}
        for d in (1, -1):
            for h in (0, 1):
                self.first[h, d] = self.send(own, (0, 0), h, 0, 2, self.step(h, 0, d))
        for d in (1, -1):
            for h in (0, 1):
                self.second[h, d, 0, 0] = self.send(own, (0, 0), h, 0, 2, self.step(h, 1, d))

    def step(self, h, phase, d):
        return (d, 0) if h == phase else (0, d)

    def at(self, ref, whole, offset, h, q, n):
        rows = pl.ds((2 * h + q) * QUARTER, n * QUARTER)
        if not whole:
            return ref.at[:, rows, :]
        return ref.at[pl.ds(self.me.col_of(*offset) * VB, VB), rows, :]

    def send(self, own, offset, h, q, n, to):
        src = self.at(own, False, offset, h, q, n) if own is not None else self.at(self.table, True, offset, h, q, n)
        return self.wire.copy(src, self.at(self.table, True, offset, h, q, n), self.me.along_col(*to))

    def middle(self):
        opposite = {}
        for d in (1, -1):
            for h in (0, 1):
                self.first[h, d].wait_recv()
                offset = self.step(h, 0, -d)
                q = 0 if d == 1 else 1
                opposite[h, d] = self.send(None, offset, h, q, 1, self.step(h, 0, d))
                for e in (1, -1):
                    self.second[h, e, -d, 0] = self.send(None, offset, h, 0, 2, self.step(h, 1, e))
        for d in (1, -1):
            for h in (0, 1):
                opposite[h, d].wait_recv()
                q = 0 if d == 1 else 1
                for e in (1, -1):
                    self.second[h, e, 2, q] = self.send(
                        None, self.step(h, 0, 2), h, q, 1, self.step(h, 1, e)
                    )

    def end(self):
        last = []
        for f in (0, -1, 1, 2):
            for e in (1, -1):
                for h in (0, 1):
                    if f == 2:
                        self.second[h, e, 2, 0].wait_recv()
                        self.second[h, e, 2, 1].wait_recv()
                    else:
                        self.second[h, e, f, 0].wait_recv()
                    a, b = self.step(h, 0, f), self.step(h, 1, -e)
                    q = 0 if e == 1 else 1
                    last.append(self.send(None, (a[0] + b[0], a[1] + b[1]), h, q, 1, self.step(h, 1, e)))
        for c in last:
            c.wait_recv()


class Exchange:
    def __init__(self, me, wire, send, recv, relay):
        self.me, self.wire, self.send, self.recv, self.relay = me, wire, send, recv, relay
        self.legs, self.got = {}, []

    def start(self, j):
        dx, dc = PLACES[j]
        me = self.me
        if dx == 2:
            for way, d in ((0, 1), (1, -1)):
                self.legs[way, dc] = self.wire.copy(
                    self.send.at[j, pl.ds(2 * way, 2)], self.relay.at[way, dc], me.along_row(d, 0)
                )
        elif (dx, dc) != (0, 0):
            self.got.append(
                self.wire.copy(self.send.at[j], self.recv.at[me.row], me.along_row(dx, dc))
            )

    def forward(self):
        me = self.me
        for dc in (0, 1):
            for way, d in ((0, 1), (1, -1)):
                self.legs[way, dc].wait_recv()
                self.got.append(
                    self.wire.copy(
                        self.relay.at[way, dc],
                        self.recv.at[me.row_of(-d, 0), pl.ds(2 * way, 2)],
                        me.along_row(d, dc),
                    )
                )

    def end(self):
        for c in self.got:
            c.wait_recv()


GATHER_COPIES = 44
EXCHANGE_COPIES = 13


def gather_kernel(
    ids, own_sku, own_store, group, fetched, requests,
    ids_v, sku_v, store_v, low, send, relay, heard, heard_s, sems, send_sem, recv_sem,
):
    me = Place()
    load_store = pltpu.make_async_copy(own_store, store_v, sems.at[0])
    load_sku = pltpu.make_async_copy(own_sku, sku_v, sems.at[1])
    load_store.start()
    load_sku.start()
    ids_v[...] = jnp.zeros_like(ids_v)
    ids_v[0:1, 0:SLOTS] = ids[...]
    peers = [me.along_row(*p) for p in PLACES[:-1]]
    meet(col_peers(me) + peers)
    wire = Wire(send_sem, recv_sem)
    asked = [
        wire.copy(ids_v, heard.at[me.row], me.along_row(*p)) for p in PLACES[:-1]
    ]
    own_ids = pltpu.make_async_copy(ids_v, heard.at[me.row], sems.at[2])
    own_ids.start()
    load_store.wait()
    low[...] = store_v[...].astype(bf16)
    gather = Gather(me, wire, low, group)
    keep_low = pltpu.make_async_copy(low, group.at[pl.ds(me.col * VB, VB)], sems.at[3])
    keep_low.start()
    for c in asked:
        c.wait_recv()
    own_ids.wait()
    to_scalars = pltpu.make_async_copy(heard, heard_s, sems.at[4])
    to_scalars.start()
    to_result = pltpu.make_async_copy(heard, requests, sems.at[5])
    to_result.start()
    load_sku.wait()
    to_scalars.wait()
    exchange = Exchange(me, wire, send, fetched, relay)
    for j, p in enumerate(PLACES):
        for t in range(CAP):
            send[j, t] = sku_v[heard_s[me.row_of(*p), 0, me.row * CAP + t]].astype(bf16)
        exchange.start(j)
    keep_sku = pltpu.make_async_copy(send.at[len(PLACES) - 1], fetched.at[me.row], sems.at[6])
    keep_sku.start()
    gather.middle()
    exchange.forward()
    gather.end()
    exchange.end()
    keep_low.wait()
    keep_sku.wait()
    to_result.wait()
    wire.finish()


STREAMS = 2
WIDTH = R // STREAMS
PART = WIDTH // 4


class Sum:
    def __init__(self, me, wire, stream, part, own_sum, far, near, far2, near2):
        self.me, self.wire, self.stream, self.part, self.own_sum = me, wire, stream, part, own_sum
        self.far, self.near, self.far2, self.near2 = far, near, far2, near2

    def axis(self, h, phase, d):
        return (d, 0) if h == phase else (0, d)

    def quarter(self, q):
        return pl.ds(self.stream * WIDTH + q * PART, PART)

    def piece(self, h, f, s):
        a, b = self.axis(h, 0, f), self.axis(h, 1, s)
        return pl.ds(self.me.col_of(a[0] + b[0], a[1] + b[1]) * VB, VB)

    def start(self, source):
        me, wire = self.me, self.wire
        self.f_far, self.f_near = {}, {}
        for n, s in enumerate((2, 1, -1, 0)):
            for h in (0, 1):
                for w, d in ((0, 1), (1, -1)):
                    q = self.quarter(2 * h + w)
                    self.f_far[h, w, n] = wire.copy(
                        source.at[self.piece(h, 2, s), q, :], self.far.at[h, w, n], me.along_col(*self.axis(h, 0, d))
                    )
        for n, s in enumerate((2, 1, -1, 0)):
            for h in (0, 1):
                for w, d in ((0, 1), (1, -1)):
                    other = 1 - w
                    self.f_near[h, w, n, other] = wire.copy(
                        source.at[self.piece(h, d, s), self.quarter(2 * h + other), :],
                        self.near.at[h, w, n, other],
                        me.along_col(*self.axis(h, 0, d)),
                    )

    def near_sums(self):
        me, wire, part = self.me, self.wire, self.part
        for n, s in enumerate((2, 1, -1, 0)):
            for h in (0, 1):
                for w, d in ((0, 1), (1, -1)):
                    self.f_far[h, w, n].wait_recv()
                    at, q = self.piece(h, d, s), self.quarter(2 * h + w)
                    part[at, q, :] = (part[at, q, :].astype(f32) + self.far[h, w, n].astype(f32)).astype(bf16)
                    self.f_near[h, w, n, w] = wire.copy(
                        part.at[at, q, :], self.near.at[h, w, n, w], me.along_col(*self.axis(h, 0, d))
                    )

    def rest(self):
        me, wire, part = self.me, self.wire, self.part
        s_far, s_near = {}, {}
        for n, s in enumerate((2, 1, -1, 0)):
            for h in (0, 1):
                at = self.piece(h, 0, s)
                for e in (0, 1):
                    for w in (0, 1):
                        self.f_near[h, w, n, e].wait_recv()
                    q = self.quarter(2 * h + e)
                    total = (
                        part[at, q, :].astype(f32)
                        + self.near[h, 0, n, e].astype(f32)
                        + self.near[h, 1, n, e].astype(f32)
                    )
                    d = 1 if e == 0 else -1
                    to = {1: me.along_col(*self.axis(h, 1, 1)), -1: me.along_col(*self.axis(h, 1, -1))}
                    if s == 2:
                        part[at, q, :] = total.astype(bf16)
                        s_far[h, e] = wire.copy(part.at[at, q, :], self.far2.at[h, e], to[d])
                    elif s == 0:
                        self.own_sum[:, q, :] = total
                    elif s == d:
                        s_far[h, e].wait_recv()
                        part[at, q, :] = (total + self.far2[h, e].astype(f32)).astype(bf16)
                        s_near[h, s, e] = wire.copy(part.at[at, q, :], self.near2.at[h, 0 if s == 1 else 1, e], to[s])
                    else:
                        part[at, q, :] = total.astype(bf16)
                        s_near[h, s, e] = wire.copy(part.at[at, q, :], self.near2.at[h, 0 if s == 1 else 1, e], to[s])
        for h in (0, 1):
            for e in (0, 1):
                s_near[h, 1, e].wait_recv()
                s_near[h, -1, e].wait_recv()
                self.own_sum[:, self.quarter(2 * h + e), :] += self.near2[h, 0, e].astype(f32) + self.near2[h, 1, e].astype(f32)


SUM_COPIES = 60


def step_kernel(
    ids, counts, grad, fetched, obs, own_store, new_store, arrived,
    part, own_sum, far, near, far2, near2, store_v, table, fetched_v, obs_v, terms, relay,
    sems, send_sem, recv_sem,
):
    me = Place()
    load_store = pltpu.make_async_copy(own_store, store_v, sems.at[0])
    load_part = pltpu.make_async_copy(grad, part, sems.at[1])
    load_store.start()
    load_part.start()
    peers = [me.along_row(*p) for p in PLACES[2:-1]]
    meet(col_peers(me) + peers)
    wire = Wire(send_sem, recv_sem)
    sums = [
        Sum(me, wire, c, part, own_sum, far.at[c], near.at[c], far2.at[c], near2.at[c]) for c in range(STREAMS)
    ]
    sums[0].start(grad)
    load_part.wait()
    load_fetched = pltpu.make_async_copy(fetched, fetched_v, sems.at[2])
    load_fetched.start()
    load_obs = pltpu.make_async_copy(obs, obs_v, sems.at[3])
    load_obs.start()
    load_store.wait()
    sums[0].near_sums()
    gathers = []
    for c in range(STREAMS):
        if c + 1 < STREAMS:
            sums[c + 1].start(grad)
        else:
            sums[c].near_sums()
        sums[c].rest()
        lanes = pl.ds(c * WIDTH, WIDTH)
        for v in range(VB):
            was = store_v[v, :, lanes]
            now = was - learn_rate * (own_sum[v, lanes, :].T + weight_decay * was)
            store_v[v, :, lanes] = now
            table[c, me.col * VB + v] = now.astype(bf16)
        gathers.append(Gather(me, wire, None, table.at[c]))
    keep_store = pltpu.make_async_copy(store_v, new_store, sems.at[4])
    keep_store.start()
    for g in gathers:
        g.middle()
    for g in gathers:
        g.end()
    load_fetched.wait()
    load_obs.wait()
    exchange = Exchange(me, wire, terms, arrived, relay)

    def block(i):
        return jnp.concatenate([table[c, i] for c in range(STREAMS)], axis=1)

    for j, p in enumerate(PLACES):
        o = me.row_of(*p)

        @pl.loop(0, CAP)
        def _(t):
            s = o * CAP + t
            x = fetched_v[o, t]
            now = obs_v.at[s]
            g = jnp.zeros((BS, R), f32)
            for k in range(0, K, 2):
                two = jnp.concatenate([block(ids[k, s]), block(ids[k + 1, s])], axis=0)
                misfit = misfit_pair(x, two, now, k)
                g = g + jnp.dot(misfit, two, preferred_element_type=f32)
            terms[j, t] = (g * (t < counts[o]).astype(f32)).astype(bf16)

        exchange.start(j)
        if j == 5:
            exchange.forward()
    keep_sku = pltpu.make_async_copy(terms.at[len(PLACES) - 1], arrived.at[me.row], sems.at[5])
    keep_sku.start()
    exchange.end()
    keep_sku.wait()
    keep_store.wait()
    wire.finish()


def last_step(requested, arrived, own, store, out, new_store):
    new_store[...] = store[...]
    row = lax.axis_index("row")
    out[...] = own[...] * (1 - learn_rate * weight_decay)

    @pl.loop(0, N_ROW)
    def _(o):
        for t in range(CAP):
            out[requested[o, 0, row * CAP + t]] -= learn_rate * arrived[o * CAP + t].astype(f32)


SMEM = pl.BlockSpec(memory_space=pltpu.SMEM)
VMEM = pl.BlockSpec(memory_space=pltpu.VMEM)
ANY = pl.BlockSpec(memory_space=pl.ANY)
params = pltpu.CompilerParams(vmem_limit_bytes=VMEM_MOST)


def remote_params(n):
    return pltpu.CompilerParams(vmem_limit_bytes=VMEM_MOST, collective_id=n, has_side_effects=True)


def local(observed, sku_ids, store_ids, live_slot_counts, sku_factors, store_factors):
    counts = live_slot_counts.reshape(N_ROW)
    own_sku = sku_factors.reshape(UB, BS, R)
    own_store = store_factors.reshape(VB, BS, R)
    store_ids = store_ids.T
    group_low, fetched, requested = pl.pallas_call(
        gather_kernel,
        out_shape=(
            jax.ShapeDtypeStruct((VG, BS, R), bf16),
            jax.ShapeDtypeStruct((N_ROW, CAP, BS, R), bf16),
            jax.ShapeDtypeStruct((N_ROW, 8, 128), jnp.int32),
        ),
        in_specs=[VMEM, ANY, ANY],
        out_specs=(ANY, ANY, ANY),
        scratch_shapes=[
            pltpu.VMEM((8, 128), jnp.int32),
            pltpu.VMEM((UB, BS, R), f32),
            pltpu.VMEM((VB, BS, R), f32),
            pltpu.VMEM((VB, BS, R), bf16),
            pltpu.VMEM((N_ROW, CAP, BS, R), bf16),
            pltpu.VMEM((2, 2, 2, BS, R), bf16),
            pltpu.VMEM((N_ROW, 8, 128), jnp.int32),
            pltpu.SMEM((N_ROW, 8, 128), jnp.int32),
            pltpu.SemaphoreType.DMA((7,)),
            pltpu.SemaphoreType.DMA((7 + GATHER_COPIES + EXCHANGE_COPIES,)),
            pltpu.SemaphoreType.DMA((7 + GATHER_COPIES + EXCHANGE_COPIES,)),
        ],
        compiler_params=remote_params(0),
        name="gather_kernel",
    )(sku_ids.reshape(1, SLOTS), own_sku, own_store)
    grad = pl.pallas_call(
        first_pass,
        out_shape=jax.ShapeDtypeStruct((VG, R, BS), bf16),
        in_specs=[SMEM, SMEM, ANY, ANY, ANY],
        out_specs=ANY,
        scratch_shapes=[
            pltpu.VMEM((VG, BS, R), bf16),
            pltpu.VMEM((VG, R, BS), f32),
            pltpu.SMEM((SLOTS + 1,), jnp.int32),
            pltpu.VMEM((DEPTH, BS, R), bf16),
            pltpu.VMEM((DEPTH, K, BS, BS), bf16),
            pltpu.VMEM((K // 2, BS, 2 * BS), bf16),
            pltpu.VMEM((VG, R, BS), bf16),
            pltpu.SemaphoreType.DMA((2, DEPTH)),
            pltpu.SemaphoreType.DMA((CHUNKS + 1,)),
        ],
        compiler_params=params,
        name="first_pass",
    )(store_ids, counts, fetched, observed, group_low)
    new_store, arrived = pl.pallas_call(
        step_kernel,
        out_shape=(
            jax.ShapeDtypeStruct((VB, BS, R), f32),
            jax.ShapeDtypeStruct((N_ROW, CAP, BS, R), bf16),
        ),
        in_specs=[SMEM, SMEM, ANY, ANY, ANY, ANY],
        out_specs=(ANY, ANY),
        scratch_shapes=[
            pltpu.VMEM((VG, R, BS), bf16),
            pltpu.VMEM((VB, R, BS), f32),
            pltpu.VMEM((STREAMS, 2, 2, RING, VB, PART, BS), bf16),
            pltpu.VMEM((STREAMS, 2, 2, RING, 2, VB, PART, BS), bf16),
            pltpu.VMEM((STREAMS, 2, 2, VB, PART, BS), bf16),
            pltpu.VMEM((STREAMS, 2, 2, 2, VB, PART, BS), bf16),
            pltpu.VMEM((VB, BS, R), f32),
            pltpu.VMEM((STREAMS, VG, BS, WIDTH), bf16),
            pltpu.VMEM((N_ROW, CAP, BS, R), bf16),
            pltpu.VMEM((SLOTS, K, BS, BS), bf16),
            pltpu.VMEM((N_ROW, CAP, BS, R), bf16),
            pltpu.VMEM((2, 2, 2, BS, R), bf16),
            pltpu.SemaphoreType.DMA((6,)),
            pltpu.SemaphoreType.DMA((STREAMS * (SUM_COPIES + GATHER_COPIES) + EXCHANGE_COPIES,)),
            pltpu.SemaphoreType.DMA((STREAMS * (SUM_COPIES + GATHER_COPIES) + EXCHANGE_COPIES,)),
        ],
        compiler_params=remote_params(1),
        name="step_kernel",
    )(store_ids, counts, grad, fetched, observed, own_store)
    part = lambda n: pl.BlockSpec((n, BS // 2, R), lambda i: (0, i, 0))
    new_sku, new_store = pl.pallas_call(
        last_step,
        out_shape=(
            jax.ShapeDtypeStruct((UB, BS, R), f32),
            jax.ShapeDtypeStruct((VB, BS, R), f32),
        ),
        grid=(2,),
        in_specs=[SMEM, part(SLOTS), part(UB), part(VB)],
        out_specs=(part(UB), part(VB)),
        compiler_params=params,
        name="last_step",
    )(requested, arrived.reshape(SLOTS, BS, R), own_sku, new_store)
    return new_sku.reshape(sku_factors.shape), new_store.reshape(store_factors.shape)


def solution(mesh):
    placed = (
        P(("row", "col"), None, None, None),
        P(("row", "col")),
        P(("row", "col"), None),
        P("row", "col", None),
        P(("row", "col"), None),
        P(("row", "col"), None),
    )
    return jax.shard_map(
        local,
        mesh=mesh,
        in_specs=placed,
        out_specs=(P(("row", "col"), None), P(("row", "col"), None)),
        check_vma=False,
    )
```

```python
import jax
import jax.numpy as jnp
from jax import lax
from jax.experimental import pallas as pl
from jax.experimental.pallas import tpu as pltpu
from jax.sharding import PartitionSpec as P

learn_rate = 0.01
weight_decay = 0.05
BS = 128
R = 256
K = 8
CAP = 4
N_ROW = 8
SLOTS = 32
UB = 16
VB = 5
VG = 80
DEPTH = 4
CHUNKS = 8
VMEM_MOST = 60 * 1024 * 1024

RING = 4
MESH = pl.DeviceIdType.MESH
NT = (((1,), (1,)), ((), ()))
f32 = jnp.float32
bf16 = jnp.bfloat16


def live_list(counts, order):
    total = jnp.int32(0)
    for o in range(N_ROW):
        for t in range(CAP):
            order[total] = o * CAP + t
            total = total + (t < counts[o]).astype(jnp.int32)
    return total


def misfit_pair(x, store, first, second, obs, k):
    two = jnp.concatenate([store[first], store[second]], axis=0)
    predicted = lax.dot_general(x, two, NT, preferred_element_type=f32)
    measured = jnp.concatenate([obs[k], obs[k + 1]], axis=1)
    return (predicted - measured.astype(f32)).astype(bf16), two


def first_pass(
    ids, counts, fetched, obs, group, out,
    store, acc, order, sku_buf, obs_buf, misfits, staged, sem, end_sem,
):
    load_store = pltpu.make_async_copy(group, store, end_sem.at[CHUNKS])
    load_store.start()
    total = live_list(counts, order)

    def copies(i):
        s = order[i]
        at = lax.rem(i, DEPTH)
        return (
            pltpu.make_async_copy(fetched.at[lax.div(s, CAP), lax.rem(s, CAP)], sku_buf.at[at], sem.at[0, at]),
            pltpu.make_async_copy(obs.at[s], obs_buf.at[at], sem.at[1, at]),
        )

    def misfit(i, k):
        s = order[i]
        at = lax.rem(i, DEPTH)
        return misfit_pair(sku_buf[at], store, ids[k, s], ids[k + 1, s], obs_buf.at[at], k)[0]

    for i in range(DEPTH - 1):

        @pl.when(i < total)
        def _():
            for c in copies(i):
                c.start()

    acc[...] = jnp.zeros_like(acc)
    load_store.wait()

    @pl.when(total > 0)
    def _():
        for c in copies(0):
            c.wait()
        for k in range(0, K, 2):
            misfits[k // 2] = misfit(0, k)

    @pl.loop(0, total)
    def _(i):
        @pl.when(i + DEPTH - 1 < total)
        def _():
            for c in copies(i + DEPTH - 1):
                c.start()

        @pl.when(i + 1 < total)
        def _():
            for c in copies(i + 1):
                c.wait()

        s = order[i]
        later = jnp.minimum(i + 1, total - 1)
        xt = sku_buf[lax.rem(i, DEPTH)].T
        gs = [jnp.dot(xt, misfits[k // 2], preferred_element_type=f32) for k in range(0, K, 2)]
        for k in range(0, K, 2):
            misfits[k // 2] = misfit(later, k)
        for k in range(0, K, 2):
            a, b = ids[k, s], ids[k + 1, s]
            acc[a] += gs[k // 2][:, :BS]
            acc[b] += gs[k // 2][:, BS:]

    n = VG // CHUNKS
    stores = []
    for q in range(CHUNKS):
        part = pl.ds(q * n, n)
        staged[part] = acc[part].astype(bf16)
        c = pltpu.make_async_copy(staged.at[part], out.at[part], end_sem.at[q])
        c.start()
        stores.append(c)
    for c in stores:
        c.wait()


class Place:
    def __init__(self):
        self.row, self.col = lax.axis_index("row"), lax.axis_index("col")
        self.x, self.core = lax.div(self.row, 2), lax.rem(self.row, 2)
        self.z, self.y = lax.div(self.col, RING), lax.rem(self.col, RING)

    def row_of(self, dx, dc):
        return lax.rem(self.x + dx + RING, RING) * 2 + (1 - self.core if dc else self.core)

    def col_of(self, dy, dz):
        return lax.rem(self.z + dz + RING, RING) * RING + lax.rem(self.y + dy + RING, RING)

    def along_row(self, dx, dc):
        return (self.row_of(dx, dc), self.col)

    def along_col(self, dy, dz):
        return (self.row, self.col_of(dy, dz))


class Wire:
    def __init__(self, send_sem, recv_sem):
        self.send_sem, self.recv_sem, self.made = send_sem, recv_sem, []

    def copy(self, src, dst, to):
        n = len(self.made)
        c = pltpu.make_async_remote_copy(
            src, dst, self.send_sem.at[n], self.recv_sem.at[n], device_id=to, device_id_type=MESH
        )
        c.start()
        self.made.append(c)
        return c

    def finish(self):
        for c in self.made:
            c.wait_send()


def meet(peers, meanwhile=None):
    barrier = pltpu.get_barrier_semaphore()
    for p in peers:
        pl.semaphore_signal(barrier, inc=1, device_id=p, device_id_type=MESH)
    if meanwhile is not None:
        meanwhile()
    pl.semaphore_wait(barrier, len(peers))


def col_peers(me):
    return [me.along_col(d, 0) for d in (1, -1)] + [me.along_col(0, d) for d in (1, -1)]


PLACES = [(2, 0), (2, 1), (1, 0), (-1, 0), (1, 1), (-1, 1), (0, 1), (0, 0)]
QUARTER = BS // 4


class Gather:
    def __init__(self, me, wire, own, table):
        self.me, self.wire, self.table = me, wire, table
        self.first, self.second = {}, {}
        for d in (1, -1):
            for h in (0, 1):
                self.first[h, d] = self.send(own, (0, 0), h, 0, 2, self.step(h, 0, d))
        for d in (1, -1):
            for h in (0, 1):
                self.second[h, d, 0, 0] = self.send(own, (0, 0), h, 0, 2, self.step(h, 1, d))

    def step(self, h, phase, d):
        return (d, 0) if h == phase else (0, d)

    def at(self, ref, whole, offset, h, q, n):
        rows = pl.ds((2 * h + q) * QUARTER, n * QUARTER)
        if not whole:
            return ref.at[:, rows, :]
        return ref.at[pl.ds(self.me.col_of(*offset) * VB, VB), rows, :]

    def send(self, own, offset, h, q, n, to):
        src = self.at(own, False, offset, h, q, n) if own is not None else self.at(self.table, True, offset, h, q, n)
        return self.wire.copy(src, self.at(self.table, True, offset, h, q, n), self.me.along_col(*to))

    def middle(self):
        opposite = {}
        for d in (1, -1):
            for h in (0, 1):
                self.first[h, d].wait_recv()
                offset = self.step(h, 0, -d)
                q = 0 if d == 1 else 1
                opposite[h, d] = self.send(None, offset, h, q, 1, self.step(h, 0, d))
                for e in (1, -1):
                    self.second[h, e, -d, 0] = self.send(None, offset, h, 0, 2, self.step(h, 1, e))
        for d in (1, -1):
            for h in (0, 1):
                opposite[h, d].wait_recv()
                q = 0 if d == 1 else 1
                for e in (1, -1):
                    self.second[h, e, 2, q] = self.send(
                        None, self.step(h, 0, 2), h, q, 1, self.step(h, 1, e)
                    )

    def end(self):
        last = []
        for f in (0, -1, 1, 2):
            for e in (1, -1):
                for h in (0, 1):
                    if f == 2:
                        self.second[h, e, 2, 0].wait_recv()
                        self.second[h, e, 2, 1].wait_recv()
                    else:
                        self.second[h, e, f, 0].wait_recv()
                    a, b = self.step(h, 0, f), self.step(h, 1, -e)
                    q = 0 if e == 1 else 1
                    last.append(self.send(None, (a[0] + b[0], a[1] + b[1]), h, q, 1, self.step(h, 1, e)))
        for c in last:
            c.wait_recv()


class Exchange:
    def __init__(self, me, wire, send, recv, relay):
        self.me, self.wire, self.send, self.recv, self.relay = me, wire, send, recv, relay
        self.legs, self.got = {}, []

    def start(self, j):
        dx, dc = PLACES[j]
        me = self.me
        if dx == 2:
            for way, d in ((0, 1), (1, -1)):
                self.legs[way, dc] = self.wire.copy(
                    self.send.at[j, pl.ds(2 * way, 2)], self.relay.at[way, dc], me.along_row(d, 0)
                )
        elif (dx, dc) != (0, 0):
            self.got.append(
                self.wire.copy(self.send.at[j], self.recv.at[me.row], me.along_row(dx, dc))
            )

    def forward(self):
        me = self.me
        for dc in (0, 1):
            for way, d in ((0, 1), (1, -1)):
                self.legs[way, dc].wait_recv()
                self.got.append(
                    self.wire.copy(
                        self.relay.at[way, dc],
                        self.recv.at[me.row_of(-d, 0), pl.ds(2 * way, 2)],
                        me.along_row(d, dc),
                    )
                )

    def end(self):
        for c in self.got:
            c.wait_recv()


GATHER_COPIES = 44
EXCHANGE_COPIES = 13


def gather_kernel(
    ids, own_sku, own_store, group, fetched, requests,
    ids_v, sku_v, store_v, low, send, relay, heard, heard_s, sems, send_sem, recv_sem,
):
    me = Place()
    load_store = pltpu.make_async_copy(own_store, store_v, sems.at[0])
    load_sku = pltpu.make_async_copy(own_sku, sku_v, sems.at[1])
    load_store.start()
    load_sku.start()
    ids_v[...] = jnp.zeros_like(ids_v)
    ids_v[0:1, 0:SLOTS] = ids[...]
    peers = [me.along_row(*p) for p in PLACES[:-1]]

    def cast():
        load_store.wait()
        low[...] = store_v[...].astype(bf16)

    meet(col_peers(me) + peers, cast)
    wire = Wire(send_sem, recv_sem)
    asked = [
        wire.copy(ids_v, heard.at[me.row], me.along_row(*p)) for p in PLACES[:-1]
    ]
    own_ids = pltpu.make_async_copy(ids_v, heard.at[me.row], sems.at[2])
    own_ids.start()
    gather = Gather(me, wire, low, group)
    keep_low = pltpu.make_async_copy(low, group.at[pl.ds(me.col * VB, VB)], sems.at[3])
    keep_low.start()
    for c in asked:
        c.wait_recv()
    own_ids.wait()
    to_scalars = pltpu.make_async_copy(heard, heard_s, sems.at[4])
    to_scalars.start()
    to_result = pltpu.make_async_copy(heard, requests, sems.at[5])
    to_result.start()
    load_sku.wait()
    to_scalars.wait()
    exchange = Exchange(me, wire, send, fetched, relay)
    for j, p in enumerate(PLACES):
        for t in range(CAP):
            send[j, t] = sku_v[heard_s[me.row_of(*p), 0, me.row * CAP + t]].astype(bf16)
        exchange.start(j)
    keep_sku = pltpu.make_async_copy(send.at[len(PLACES) - 1], fetched.at[me.row], sems.at[6])
    keep_sku.start()
    gather.middle()
    exchange.forward()
    gather.end()
    exchange.end()
    keep_low.wait()
    keep_sku.wait()
    to_result.wait()
    wire.finish()


def quarter(q):
    return pl.ds(q * (R // 4), R // 4)


class Sum:
    def __init__(self, me, wire, part, own_sum, far, near, far2, near2):
        self.me, self.wire, self.part, self.own_sum = me, wire, part, own_sum
        self.far, self.near, self.far2, self.near2 = far, near, far2, near2

    def axis(self, h, phase, d):
        return (d, 0) if h == phase else (0, d)

    def piece(self, h, f, s):
        a, b = self.axis(h, 0, f), self.axis(h, 1, s)
        return pl.ds(self.me.col_of(a[0] + b[0], a[1] + b[1]) * VB, VB)

    def start(self, source):
        me, wire = self.me, self.wire
        self.f_far, self.f_near = {}, {}
        for n, s in enumerate((2, 1, -1, 0)):
            for h in (0, 1):
                for w, d in ((0, 1), (1, -1)):
                    q = quarter(2 * h + w)
                    self.f_far[h, w, n] = wire.copy(
                        source.at[self.piece(h, 2, s), q, :], self.far.at[h, w, n], me.along_col(*self.axis(h, 0, d))
                    )
        for n, s in enumerate((2, 1, -1, 0)):
            for h in (0, 1):
                for w, d in ((0, 1), (1, -1)):
                    other = 1 - w
                    self.f_near[h, w, n, other] = wire.copy(
                        source.at[self.piece(h, d, s), quarter(2 * h + other), :],
                        self.near.at[h, w, n, other],
                        me.along_col(*self.axis(h, 0, d)),
                    )

    def rest(self):
        me, wire, part = self.me, self.wire, self.part
        for n, s in enumerate((2, 1, -1, 0)):
            for h in (0, 1):
                for w, d in ((0, 1), (1, -1)):
                    self.f_far[h, w, n].wait_recv()
                    at, q = self.piece(h, d, s), quarter(2 * h + w)
                    part[at, q, :] = (part[at, q, :].astype(f32) + self.far[h, w, n].astype(f32)).astype(bf16)
                    self.f_near[h, w, n, w] = wire.copy(
                        part.at[at, q, :], self.near.at[h, w, n, w], me.along_col(*self.axis(h, 0, d))
                    )
        s_far, s_near = {}, {}
        for n, s in enumerate((2, 1, -1, 0)):
            for h in (0, 1):
                at = self.piece(h, 0, s)
                for e in (0, 1):
                    for w in (0, 1):
                        self.f_near[h, w, n, e].wait_recv()
                    q = quarter(2 * h + e)
                    total = (
                        part[at, q, :].astype(f32)
                        + self.near[h, 0, n, e].astype(f32)
                        + self.near[h, 1, n, e].astype(f32)
                    )
                    d = 1 if e == 0 else -1
                    to = {1: me.along_col(*self.axis(h, 1, 1)), -1: me.along_col(*self.axis(h, 1, -1))}
                    if s == 2:
                        part[at, q, :] = total.astype(bf16)
                        s_far[h, e] = wire.copy(part.at[at, q, :], self.far2.at[h, e], to[d])
                    elif s == 0:
                        self.own_sum[:, q, :] = total
                    elif s == d:
                        s_far[h, e].wait_recv()
                        part[at, q, :] = (total + self.far2[h, e].astype(f32)).astype(bf16)
                        s_near[h, s, e] = wire.copy(part.at[at, q, :], self.near2.at[h, 0 if s == 1 else 1, e], to[s])
                    else:
                        part[at, q, :] = total.astype(bf16)
                        s_near[h, s, e] = wire.copy(part.at[at, q, :], self.near2.at[h, 0 if s == 1 else 1, e], to[s])
        for h in (0, 1):
            for e in (0, 1):
                s_near[h, 1, e].wait_recv()
                s_near[h, -1, e].wait_recv()
                self.own_sum[:, quarter(2 * h + e), :] += self.near2[h, 0, e].astype(f32) + self.near2[h, 1, e].astype(f32)


SUM_COPIES = 60


def step_kernel(
    ids, counts, grad, fetched, obs, own_store, new_store, arrived,
    part, own_sum, far, near, far2, near2, store_v, table, fetched_v, obs_v, terms, relay,
    sems, send_sem, recv_sem,
):
    me = Place()
    load_store = pltpu.make_async_copy(own_store, store_v, sems.at[0])
    load_part = pltpu.make_async_copy(grad, part, sems.at[1])
    load_store.start()
    load_part.start()
    peers = [me.along_row(*p) for p in PLACES[2:-1]]
    meet(col_peers(me) + peers)
    wire = Wire(send_sem, recv_sem)
    total = Sum(me, wire, part, own_sum, far, near, far2, near2)
    total.start(grad)
    load_part.wait()
    load_fetched = pltpu.make_async_copy(fetched, fetched_v, sems.at[2])
    load_fetched.start()
    load_obs = pltpu.make_async_copy(obs, obs_v, sems.at[3])
    load_obs.start()
    total.rest()
    load_store.wait()
    for v in range(VB):
        was = store_v[v]
        now = was - learn_rate * (own_sum[v].T + weight_decay * was)
        store_v[v] = now
        table[me.col * VB + v] = now.astype(bf16)
    gather = Gather(me, wire, None, table)
    keep_store = pltpu.make_async_copy(store_v, new_store, sems.at[4])
    keep_store.start()
    gather.middle()
    gather.end()
    load_fetched.wait()
    load_obs.wait()
    exchange = Exchange(me, wire, terms, arrived, relay)
    for j, p in enumerate(PLACES):
        o = me.row_of(*p)

        @pl.loop(0, CAP)
        def _(t):
            s = o * CAP + t
            x = fetched_v[o, t]
            now = obs_v.at[s]
            g = jnp.zeros((BS, R), f32)
            for k in range(0, K, 2):
                misfit, two = misfit_pair(x, table, ids[k, s], ids[k + 1, s], now, k)
                g = g + jnp.dot(misfit, two, preferred_element_type=f32)
            terms[j, t] = (g * (t < counts[o]).astype(f32)).astype(bf16)

        exchange.start(j)
        if j == 5:
            exchange.forward()
    keep_sku = pltpu.make_async_copy(terms.at[len(PLACES) - 1], arrived.at[me.row], sems.at[5])
    keep_sku.start()
    exchange.end()
    keep_sku.wait()
    keep_store.wait()
    wire.finish()


def last_step(requested, arrived, own, store, out, new_store):
    new_store[...] = store[...]
    row = lax.axis_index("row")
    out[...] = own[...] * (1 - learn_rate * weight_decay)

    @pl.loop(0, N_ROW)
    def _(o):
        for t in range(CAP):
            out[requested[o, 0, row * CAP + t]] -= learn_rate * arrived[o * CAP + t].astype(f32)


SMEM = pl.BlockSpec(memory_space=pltpu.SMEM)
VMEM = pl.BlockSpec(memory_space=pltpu.VMEM)
ANY = pl.BlockSpec(memory_space=pl.ANY)
params = pltpu.CompilerParams(vmem_limit_bytes=VMEM_MOST)


def remote_params(n):
    return pltpu.CompilerParams(vmem_limit_bytes=VMEM_MOST, collective_id=n, has_side_effects=True)


def local(observed, sku_ids, store_ids, live_slot_counts, sku_factors, store_factors):
    counts = live_slot_counts.reshape(N_ROW)
    own_sku = sku_factors.reshape(UB, BS, R)
    own_store = store_factors.reshape(VB, BS, R)
    store_ids = store_ids.T
    group_low, fetched, requested = pl.pallas_call(
        gather_kernel,
        out_shape=(
            jax.ShapeDtypeStruct((VG, BS, R), bf16),
            jax.ShapeDtypeStruct((N_ROW, CAP, BS, R), bf16),
            jax.ShapeDtypeStruct((N_ROW, 8, 128), jnp.int32),
        ),
        in_specs=[VMEM, ANY, ANY],
        out_specs=(ANY, ANY, ANY),
        scratch_shapes=[
            pltpu.VMEM((8, 128), jnp.int32),
            pltpu.VMEM((UB, BS, R), f32),
            pltpu.VMEM((VB, BS, R), f32),
            pltpu.VMEM((VB, BS, R), bf16),
            pltpu.VMEM((N_ROW, CAP, BS, R), bf16),
            pltpu.VMEM((2, 2, 2, BS, R), bf16),
            pltpu.VMEM((N_ROW, 8, 128), jnp.int32),
            pltpu.SMEM((N_ROW, 8, 128), jnp.int32),
            pltpu.SemaphoreType.DMA((7,)),
            pltpu.SemaphoreType.DMA((7 + GATHER_COPIES + EXCHANGE_COPIES,)),
            pltpu.SemaphoreType.DMA((7 + GATHER_COPIES + EXCHANGE_COPIES,)),
        ],
        compiler_params=remote_params(0),
        name="gather_kernel",
    )(sku_ids.reshape(1, SLOTS), own_sku, own_store)
    grad = pl.pallas_call(
        first_pass,
        out_shape=jax.ShapeDtypeStruct((VG, R, BS), bf16),
        in_specs=[SMEM, SMEM, ANY, ANY, ANY],
        out_specs=ANY,
        scratch_shapes=[
            pltpu.VMEM((VG, BS, R), bf16),
            pltpu.VMEM((VG, R, BS), f32),
            pltpu.SMEM((SLOTS + 1,), jnp.int32),
            pltpu.VMEM((DEPTH, BS, R), bf16),
            pltpu.VMEM((DEPTH, K, BS, BS), bf16),
            pltpu.VMEM((K // 2, BS, 2 * BS), bf16),
            pltpu.VMEM((VG, R, BS), bf16),
            pltpu.SemaphoreType.DMA((2, DEPTH)),
            pltpu.SemaphoreType.DMA((CHUNKS + 1,)),
        ],
        compiler_params=params,
        name="first_pass",
    )(store_ids, counts, fetched, observed, group_low)
    new_store, arrived = pl.pallas_call(
        step_kernel,
        out_shape=(
            jax.ShapeDtypeStruct((VB, BS, R), f32),
            jax.ShapeDtypeStruct((N_ROW, CAP, BS, R), bf16),
        ),
        in_specs=[SMEM, SMEM, ANY, ANY, ANY, ANY],
        out_specs=(ANY, ANY),
        scratch_shapes=[
            pltpu.VMEM((VG, R, BS), bf16),
            pltpu.VMEM((VB, R, BS), f32),
            pltpu.VMEM((2, 2, RING, VB, R // 4, BS), bf16),
            pltpu.VMEM((2, 2, RING, 2, VB, R // 4, BS), bf16),
            pltpu.VMEM((2, 2, VB, R // 4, BS), bf16),
            pltpu.VMEM((2, 2, 2, VB, R // 4, BS), bf16),
            pltpu.VMEM((VB, BS, R), f32),
            pltpu.VMEM((VG, BS, R), bf16),
            pltpu.VMEM((N_ROW, CAP, BS, R), bf16),
            pltpu.VMEM((SLOTS, K, BS, BS), bf16),
            pltpu.VMEM((N_ROW, CAP, BS, R), bf16),
            pltpu.VMEM((2, 2, 2, BS, R), bf16),
            pltpu.SemaphoreType.DMA((6,)),
            pltpu.SemaphoreType.DMA((SUM_COPIES + GATHER_COPIES + EXCHANGE_COPIES,)),
            pltpu.SemaphoreType.DMA((SUM_COPIES + GATHER_COPIES + EXCHANGE_COPIES,)),
        ],
        compiler_params=remote_params(1),
        name="step_kernel",
    )(store_ids, counts, grad, fetched, observed, own_store)
    part = lambda n: pl.BlockSpec((n, BS // 2, R), lambda i: (0, i, 0))
    new_sku, new_store = pl.pallas_call(
        last_step,
        out_shape=(
            jax.ShapeDtypeStruct((UB, BS, R), f32),
            jax.ShapeDtypeStruct((VB, BS, R), f32),
        ),
        grid=(2,),
        in_specs=[SMEM, part(SLOTS), part(UB), part(VB)],
        out_specs=(part(UB), part(VB)),
        compiler_params=params,
        name="last_step",
    )(requested, arrived.reshape(SLOTS, BS, R), own_sku, new_store)
    return new_sku.reshape(sku_factors.shape), new_store.reshape(store_factors.shape)


def solution(mesh):
    placed = (
        P(("row", "col"), None, None, None),
        P(("row", "col")),
        P(("row", "col"), None),
        P("row", "col", None),
        P(("row", "col"), None),
        P(("row", "col"), None),
    )
    return jax.shard_map(
        local,
        mesh=mesh,
        in_specs=placed,
        out_specs=(P(("row", "col"), None), P(("row", "col"), None)),
        check_vma=False,
    )
```
